32 devices in a mesh: team: 4 (over x, core), blk: 8 (over z, y).
Axes of the slice: x: 2, y: 2, z: 4, core: 2. Of those that a mesh axis runs over, the one named last changes fastest.
Arguments:
- queries: bfloat16 [4096, 512], P(('blk', 'team')), may hold values from -6 to 6
- keys: bfloat16 [4096, 64], P(('blk', 'team')), may hold values from -6 to 6
- values: bfloat16 [4096, 64], P(('blk', 'team')), may hold values from -6 to 6
- attn_out: bfloat16 [4096, 512], P(('blk', 'team')), may hold values from -6 to 6
- out_grad: bfloat16 [4096, 512], P(('blk', 'team')), may hold values from -18 to 18
- log_norm: float32 [8, 4096], P(None, ('blk', 'team')), may hold values from 0 to 10
- doc_start: int32 [4096], P(('blk', 'team')), may hold values from 0 to 4095, as said below
Outputs:
- query_grad: bfloat16 [4096, 512], P(('blk', 'team'))
- key_grad: bfloat16 [4096, 64], P(('blk', 'team'))
- value_grad: bfloat16 [4096, 64], P(('blk', 'team'))
The draws below stay inside these ranges and needn't reach their ends.
Inputs may be any that keep to these rules, and one draw needn't show every extreme that they name: `doc_start`: documents are runs of consecutive positions, each at most 512 long and one exactly 512; every value is the first position of its run, never after the position itself.
All inputs are finite; a program needn't handle non-finite values.
Results may differ from the reference program's by a relative error of at most 0.0058.
Values may be sent and summed in bfloat16 or wider, within the bound.
No kernel may reach another device: no remote copies, remote signals or barrier semaphores. Data moves between devices by JAX's collectives and lax.ppermute only.
A program may use at most 64 MiB of HBM per device.

```python
import math
import jax
import jax.numpy as jnp
from jax import lax

HEADS = 8
HEAD_DIM = 64
SEQ = 4096
MAXDOC = 512


def document_begins(key):
    overall = SEQ
    longest = MAXDOC
    half = longest // 2
    front = 3 * half
    tail_first = overall - 3 * half
    tail_second = overall - half
    key_lengths = jax.random.fold_in(key, 11)
    lengths = jax.random.randint(key_lengths, (overall,), 1, longest + 1)
    finish = jnp.cumsum(lengths)
    begins = finish - lengths
    positions = jnp.arange(overall)
    shifted = jnp.maximum(positions - front, 0)
    owners = jnp.searchsorted(finish, shifted, side='right')
    middle = front + begins[owners]
    result = jnp.where(positions < half, 0, jnp.where(positions < front, half, middle))
    result = jnp.where(positions >= tail_first, jnp.maximum(result, tail_first), result)
    result = jnp.where(positions >= tail_second, tail_second, result)
    return result.astype(jnp.int32)


def draw_doc_start(key, part):
    return document_begins(key)


def draw_log_norm(key, part):
    begins = document_begins(key)
    counts = (jnp.arange(SEQ) - begins + 1).astype(jnp.float32)
    key_noise = jax.random.fold_in(key, 13)
    noise = jax.random.uniform(key_noise, (HEADS, SEQ), jnp.float32, 0.2, 1.0)
    return (jnp.log(counts)[None, :] + noise).astype(jnp.float32)


def block_levels(stream_key, dims, cuts, low, largest):
    def one(position, blocks):
        steps = jax.random.uniform(jax.random.fold_in(jax.random.fold_in(stream_key, 6), position), (blocks,), jnp.float32, low / len(cuts), largest / len(cuts))
        return jnp.repeat(jnp.exp(steps), dims[position] // blocks).reshape((-1,) + (1,) * (len(dims) - position - 1))

    gain = one(*cuts[0])
    for cut in cuts[1:]:
        gain = gain * one(*cut)
    return gain


def bell_draw(key, extent, width, most, shards=(), held_as=jnp.bfloat16):
    drawn = jax.random.normal(key, extent, jnp.float32) * width
    if len(shards) > 0:
        drawn = block_levels(key, extent, shards, -0.22, 0.18) * drawn
    return jnp.clip(drawn, min=-most, max=most).astype(held_as)


def setup_inputs(seed: int = 0) -> dict:
    arg_keys = jax.random.split(jax.random.key(seed), 8)
    return {
        "queries": bell_draw(arg_keys[0], (SEQ, HEADS * HEAD_DIM), 1.0, 6.0, ((0, 32),)),
        "keys": bell_draw(arg_keys[1], (SEQ, HEAD_DIM), 1.0, 6.0, ((0, 32),)),
        "values": bell_draw(arg_keys[2], (SEQ, HEAD_DIM), 1.0, 6.0, ((0, 32),)),
        "attn_out": bell_draw(arg_keys[3], (SEQ, HEADS * HEAD_DIM), 1.0, 6.0, ((0, 32),)),
        "out_grad": bell_draw(arg_keys[4], (SEQ, HEADS * HEAD_DIM), 3.0, 18.0, ((0, 32),)),
        "log_norm": draw_log_norm(jax.random.fold_in(arg_keys[7], 71), 0),
        "doc_start": draw_doc_start(jax.random.fold_in(arg_keys[7], 71), 0),
    }


def visible_pairs(query_pos, query_begin, key_pos):
    return (key_pos[None, :] <= query_pos[:, None]) & (key_pos[None, :] >= query_begin[:, None])

def grad_terms(query_rows, grad_rows, log_rows, delta_rows, key_block, value_block, allowed):
    row_count = query_rows.shape[0]
    head_count = log_rows.shape[0]
    head_width = key_block.shape[1]
    factor = 1.0 / jnp.sqrt(jnp.float32(head_width))
    query_heads = query_rows.reshape(row_count, head_count, head_width).astype(jnp.float32)
    grad_heads = grad_rows.reshape(row_count, head_count, head_width).astype(jnp.float32)
    key_wide = key_block.astype(jnp.float32)
    value_wide = value_block.astype(jnp.float32)
    scores = jnp.einsum('rhd,cd->hrc', query_heads, key_wide) * factor
    weights = jnp.where(allowed[None], jnp.exp(scores - log_rows[:, :, None]), jnp.float32(0.0))
    weights_low = lax.optimization_barrier(weights.astype(jnp.bfloat16)).astype(jnp.float32)
    value_grad = jnp.einsum('hrc,rhd->cd', weights_low, grad_heads)
    prob_grad = jnp.einsum('rhd,cd->hrc', grad_heads, value_wide)
    score_grad = (weights * (prob_grad - delta_rows[:, :, None])).astype(jnp.bfloat16)
    score_wide = lax.optimization_barrier(score_grad).astype(jnp.float32)
    query_grad = jnp.einsum('hrc,cd->rhd', score_wide, key_wide).reshape(row_count, head_count * head_width) * factor
    key_grad = jnp.einsum('hrc,rhd->cd', score_wide, query_heads) * factor
    return (query_grad, key_grad, value_grad)

def reference(queries, keys, values, attn_out, out_grad, log_norm, doc_start):
    sequence = queries.shape[0]
    delta = jnp.einsum('rhd,rhd->hr', out_grad.reshape(sequence, HEADS, HEAD_DIM).astype(jnp.float32), attn_out.reshape(sequence, HEADS, HEAD_DIM).astype(jnp.float32))
    block_rows = math.gcd(sequence, 512)
    window = min(sequence, block_rows + MAXDOC)
    positions = jnp.arange(sequence, dtype=jnp.int32)

    def visit(carried, block_index):
        key_acc, value_acc = carried
        first = (block_index * block_rows).astype(jnp.int32)
        key_first = jnp.clip(first + block_rows - window, 0, sequence - window).astype(jnp.int32)
        query_rows = lax.dynamic_slice_in_dim(queries, first, block_rows, 0)
        grad_rows = lax.dynamic_slice_in_dim(out_grad, first, block_rows, 0)
        log_rows = lax.dynamic_slice_in_dim(log_norm, first, block_rows, 1)
        delta_rows = lax.dynamic_slice_in_dim(delta, first, block_rows, 1)
        query_pos = lax.dynamic_slice_in_dim(positions, first, block_rows, 0)
        query_begin = lax.dynamic_slice_in_dim(doc_start, first, block_rows, 0)
        key_pos = lax.dynamic_slice_in_dim(positions, key_first, window, 0)
        key_block = lax.dynamic_slice_in_dim(keys, key_first, window, 0)
        value_block = lax.dynamic_slice_in_dim(values, key_first, window, 0)
        allowed = visible_pairs(query_pos, query_begin, key_pos)
        query_term, key_term, value_term = grad_terms(query_rows, grad_rows, log_rows, delta_rows, key_block, value_block, allowed)
        key_acc = lax.dynamic_update_slice_in_dim(key_acc, lax.dynamic_slice_in_dim(key_acc, key_first, window, 0) + key_term, key_first, 0)
        value_acc = lax.dynamic_update_slice_in_dim(value_acc, lax.dynamic_slice_in_dim(value_acc, key_first, window, 0) + value_term, key_first, 0)
        return ((key_acc, value_acc), query_term)
    start_acc = (jnp.zeros((sequence, HEAD_DIM), jnp.float32), jnp.zeros((sequence, HEAD_DIM), jnp.float32))
    (key_acc, value_acc), query_grad = lax.scan(visit, start_acc, jnp.arange(sequence // block_rows, dtype=jnp.int32))
    query_grad = query_grad.reshape(sequence, HEADS * HEAD_DIM)
    return (query_grad.astype(jnp.bfloat16), key_acc.astype(jnp.bfloat16), value_acc.astype(jnp.bfloat16))
```

```python
import math

import jax
import jax.numpy as jnp
from jax import lax
from jax.experimental import pallas as pl
from jax.experimental.pallas import tpu as pltpu
from jax.sharding import PartitionSpec as P

NT = (((1,), (1,)), ((), ()))
NN = (((1,), (0,)), ((), ()))


def passed_along(x, axis, by):
    count = lax.axis_size(axis)
    pairs = [(i, i + by) for i in range(count) if 0 <= i + by < count]
    return lax.ppermute(x, axis, pairs)


def dot(a, b, dims):
    return lax.dot_general(a, b, dims, preferred_element_type=jnp.float32)


def grad_kernel(rows, team, heads, width):
    lanes = 2 * width
    window = (team + 1) * rows
    factor = 1.0 / math.sqrt(width)

    def body(q_ref, g_ref, o_ref, log_ref, begin_ref, own_ref, near_ref, *rest):
        dq_ref, own_out, near_out = rest[:3]
        piece_refs = rest[3 : 3 + team - 1]
        kv_ref, acc_ref = rest[3 + team - 1 :]
        spot = lax.axis_index("team")
        place = lax.axis_index("blk") * team + spot
        kv_ref[: team * rows] = near_ref[...]
        kv_ref[team * rows :] = own_ref[...]
        kv = kv_ref[pl.ds(pl.multiple_of(spot * rows, rows), window), :]
        low_lane = lax.broadcasted_iota(jnp.int32, (window, lanes), 1) < width
        none = jnp.zeros_like(kv)
        k_low = jnp.where(low_lane, kv * jnp.asarray(factor, kv.dtype), none)
        v_high = jnp.where(low_lane, none, kv)
        turned_k = jnp.concatenate([k_low[:, width:], k_low[:, :width]], 1)
        turned_v = jnp.concatenate([v_high[:, width:], v_high[:, :width]], 1)
        key_halves = (k_low, turned_k)
        value_halves = (turned_v, v_high)
        key_flip = k_low.astype(jnp.float32).T[:width].astype(kv.dtype)
        key_pos = lax.broadcasted_iota(jnp.int32, (window, rows), 0)
        row_pos = lax.broadcasted_iota(jnp.int32, (window, rows), 1) + team * rows
        begin = begin_ref[...] - (place - team) * rows
        allowed = (key_pos <= row_pos) & (key_pos >= begin)
        prod = g_ref[...].astype(jnp.float32) * o_ref[...].astype(jnp.float32)
        feature = lax.broadcasted_iota(jnp.int32, (heads, heads * width), 1)
        head_of = lax.broadcasted_iota(jnp.int32, (heads, heads * width), 0)
        pick = (feature // width == head_of).astype(jnp.float32)
        delta = lax.dot_general(
            pick,
            prod,
            NT,
            precision=lax.Precision.HIGHEST,
            preferred_element_type=jnp.float32,
        )
        row_low = lax.broadcasted_iota(jnp.int32, (rows, lanes), 1) < width
        for pair in range(heads // 2):
            span = slice(pair * lanes, (pair + 1) * lanes)
            q_pair = q_ref[:, span]
            g_pair = g_ref[:, span]
            q_turn = jnp.concatenate([q_pair[:, width:], q_pair[:, :width]], 1)
            g_turn = jnp.concatenate([g_pair[:, width:], g_pair[:, :width]], 1)
            blank = jnp.zeros_like(q_pair)
            stack = jnp.concatenate(
                [
                    jnp.where(row_low, q_pair, blank),
                    jnp.where(row_low, q_turn, blank),
                    jnp.where(row_low, blank, g_turn),
                    jnp.where(row_low, blank, g_pair),
                ],
                0,
            )
            probs, grads, flips = [], [], []
            for half in range(2):
                head = 2 * pair + half
                scores = dot(key_halves[half], q_pair, NT)
                shifted = scores - log_ref[head : head + 1, :]
                weights = jnp.exp(jnp.where(allowed, shifted, -jnp.inf))
                prob_grad = dot(value_halves[half], g_pair, NT)
                score_grad = weights * (prob_grad - delta[head : head + 1, :])
                low = score_grad.astype(jnp.bfloat16)
                probs.append(weights.astype(jnp.bfloat16))
                grads.append(low)
                flips.append(dot(key_flip, low, NN))
            term = dot(jnp.concatenate(grads + probs, 1), stack, NN)
            if pair == 0:
                acc_ref[...] = term
            else:
                acc_ref[...] += term
            dq_ref[:, span] = jnp.concatenate(flips, 0).T.astype(dq_ref.dtype)
        scale = jnp.where(row_low, jnp.float32(factor), jnp.float32(1.0))
        near_out[...] = acc_ref[:rows] * scale
        own_out[...] = acc_ref[team * rows :] * scale
        for step in range(1, team):
            ahead = ((spot ^ step) - spot + team) % team
            part = acc_ref[pl.ds(pl.multiple_of(ahead * rows, rows), rows), :]
            piece_refs[step - 1][...] = (part * scale).astype(jnp.bfloat16)

    self_shape = jax.ShapeDtypeStruct((rows, lanes), jnp.float32)
    piece_shape = jax.ShapeDtypeStruct((rows, lanes), jnp.bfloat16)
    return pl.pallas_call(
        body,
        out_shape=[
            jax.ShapeDtypeStruct((rows, heads * width), jnp.bfloat16),
            self_shape,
            self_shape,
        ]
        + [piece_shape] * (team - 1),
        scratch_shapes=[
            pltpu.VMEM((2 * team * rows, lanes), jnp.bfloat16),
            pltpu.VMEM((window, lanes), jnp.float32),
        ],
    )


def per_device(queries, keys, values, attn_out, out_grad, log_norm, doc_start):
    rows = queries.shape[0]
    heads = log_norm.shape[0]
    width = keys.shape[1]
    team = lax.axis_size("team")
    spot = lax.axis_index("team")
    packed = jnp.concatenate([keys, values], 1)
    own = lax.all_gather(packed, "team", axis=0, tiled=False)
    near = passed_along(own, "blk", 1)
    outs = grad_kernel(rows, team, heads, width)(
        queries,
        out_grad,
        attn_out,
        log_norm,
        doc_start.reshape(1, rows),
        own.reshape(team * rows, 2 * width),
        near.reshape(team * rows, 2 * width),
    )
    query_grad, own_sum, near_sum = outs[:3]
    nothing = jnp.float32(0.0)
    for step in range(1, team):
        got = lax.ppermute(outs[2 + step], "team", [(i, i ^ step) for i in range(team)])
        got = got.astype(jnp.float32)
        later = (spot ^ step) > spot
        own_sum = own_sum + jnp.where(later, got, nothing)
        near_sum = near_sum + jnp.where(later, nothing, got)
    back = passed_along(near_sum.astype(jnp.bfloat16), "blk", -1)
    total = (own_sum + back.astype(jnp.float32)).astype(jnp.bfloat16)
    return (query_grad, total[:, :width], total[:, width:])


def solution(mesh):
    row = P(("blk", "team"), None)
    return jax.shard_map(
        per_device,
        mesh=mesh,
        in_specs=(row, row, row, row, row, P(None, ("blk", "team")), P(("blk", "team"))),
        out_specs=(row, row, row),
        check_vma=False,
    )
```

```python
import math

import jax
import jax.numpy as jnp
from jax import lax
from jax.experimental import pallas as pl
from jax.experimental.pallas import tpu as pltpu
from jax.sharding import PartitionSpec as P

NT = (((1,), (1,)), ((), ()))
NN = (((1,), (0,)), ((), ()))


def around(x, axis, by):
    count = lax.axis_size(axis)
    return lax.ppermute(x, axis, [(i, (i + by) % count) for i in range(count)])


def exchanged(x, axis, step):
    count = lax.axis_size(axis)
    return lax.ppermute(x, axis, [(i, i ^ step) for i in range(count)])


def dot(a, b, dims):
    return lax.dot_general(a, b, dims, preferred_element_type=jnp.float32)


def half_turn(x, width):
    return jnp.concatenate([x[:, width:], x[:, :width]], 1)


def tile_terms(kv_cols, q_ref, g_ref, log_ref, begin_ref, delta, first, causal, acc_ref, emit):
    lanes, total = kv_cols.shape
    width = lanes // 2
    rows = q_ref.shape[0]
    team = total // rows
    heads = log_ref.shape[0]
    factor = 1.0 / math.sqrt(width)
    spot = lax.axis_index("team")
    kv = kv_cols.T
    low_key = lax.broadcasted_iota(jnp.int32, (total, lanes), 1) < width
    none = jnp.zeros_like(kv)
    small = jnp.asarray(factor, kv.dtype)
    k_low = jnp.where(low_key, kv * small, none)
    v_high = jnp.where(low_key, none, kv)
    key_halves = (k_low, half_turn(k_low, width))
    value_halves = (half_turn(v_high, width), v_high)
    key_flip = kv_cols[:width] * small
    slabs = []
    for step in range(team):
        inside = lax.broadcasted_iota(jnp.int32, (rows, rows), 0)
        slabs.append(inside + (first + (spot ^ step) * rows))
    key_pos = jnp.concatenate(slabs, 0)
    allowed = key_pos >= begin_ref[...]
    if causal:
        allowed &= key_pos <= lax.broadcasted_iota(jnp.int32, (total, rows), 1)
    row_low = lax.broadcasted_iota(jnp.int32, (rows, lanes), 1) < width
    for pair in range(heads // 2):
        span = slice(pair * lanes, (pair + 1) * lanes)
        q_pair = q_ref[:, span]
        g_pair = g_ref[:, span]
        blank = jnp.zeros_like(q_pair)
        stack = jnp.concatenate(
            [
                jnp.where(row_low, q_pair, blank),
                jnp.where(row_low, half_turn(q_pair, width), blank),
                jnp.where(row_low, blank, half_turn(g_pair, width)),
                jnp.where(row_low, blank, g_pair),
            ],
            0,
        )
        probs, grads, flips = [], [], []
        for half in range(2):
            head = 2 * pair + half
            scores = dot(key_halves[half], q_pair, NT)
            shifted = scores - log_ref[head : head + 1, :]
            weights = jnp.exp(jnp.where(allowed, shifted, -jnp.inf))
            prob_grad = dot(value_halves[half], g_pair, NT)
            score_grad = weights * (prob_grad - delta[head : head + 1, :])
            low = score_grad.astype(jnp.bfloat16)
            probs.append(weights.astype(jnp.bfloat16))
            grads.append(low)
            flips.append(dot(key_flip, low, NN))
        term = dot(jnp.concatenate(grads + probs, 1), stack, NN)
        if pair == 0:
            acc_ref[...] = term
        else:
            acc_ref[...] += term
        emit(pair, jnp.concatenate(flips, 0))


def slab_of(acc_ref, step, rows, width):
    part = acc_ref[step * rows : (step + 1) * rows, :].T
    upper = lax.broadcasted_iota(jnp.int32, part.shape, 0) < width
    return part * jnp.where(upper, jnp.float32(1.0 / math.sqrt(width)), jnp.float32(1.0))


def own_body(q_ref, g_ref, o_ref, log_ref, begin_ref, kv_ref, *rest):
    dq_ref, delta_ref, self_ref, *more = rest
    piece_refs, acc_ref = more[:-1], more[-1]
    rows, features = q_ref.shape
    heads = log_ref.shape[0]
    width = features // heads
    prod = g_ref[...].astype(jnp.float32) * o_ref[...].astype(jnp.float32)
    feature = lax.broadcasted_iota(jnp.int32, (heads, features), 1)
    head_of = lax.broadcasted_iota(jnp.int32, (heads, features), 0)
    pick = (feature // width == head_of).astype(jnp.float32)
    delta = lax.dot_general(
        pick, prod, NT, precision=lax.Precision.HIGHEST, preferred_element_type=jnp.float32
    )
    delta_ref[...] = delta

    def emit(pair, flips):
        dq_ref[pair * 2 * width : (pair + 1) * 2 * width, :] = flips

    first = -lax.axis_index("team") * rows
    tile_terms(kv_ref[...], q_ref, g_ref, log_ref, begin_ref, delta, first, True, acc_ref, emit)
    self_ref[...] = slab_of(acc_ref, 0, rows, width)
    for step in range(1, len(piece_refs) + 1):
        piece_refs[step - 1][...] = slab_of(acc_ref, step, rows, width).astype(jnp.bfloat16)


def near_body(team, q_ref, g_ref, log_ref, begin_ref, kv_ref, part_ref, delta_ref, *rest):
    own_refs, more = rest[: team - 1], rest[team - 1 :]
    dq_ref, self_ref = more[:2]
    piece_refs, acc_ref = more[2:-1], more[-1]
    rows, features = q_ref.shape
    width = features // log_ref.shape[0]
    spot = lax.axis_index("team")

    def emit(pair, flips):
        span = slice(pair * 2 * width, (pair + 1) * 2 * width)
        dq_ref[:, span] = (part_ref[span, :] + flips).T.astype(dq_ref.dtype)

    first = -(spot + team) * rows
    tile_terms(
        kv_ref[...], q_ref, g_ref, log_ref, begin_ref, delta_ref[...], first, False, acc_ref, emit
    )
    self_ref[...] = slab_of(acc_ref, 0, rows, width)
    for step in range(1, team):
        mine = slab_of(acc_ref, step, rows, width).astype(jnp.bfloat16)
        later = jnp.full(mine.shape, (spot ^ step) > spot)
        piece_refs[step - 1][...] = jnp.where(later, mine, own_refs[step - 1][...])


def in_vmem(count):
    return [pl.BlockSpec(memory_space=pltpu.VMEM) for _ in range(count)]


def held(*arrays):
    return [pltpu.with_memory_space_constraint(x, pltpu.VMEM) for x in arrays]


def per_device(queries, keys, values, attn_out, out_grad, log_norm, doc_start):
    rows, features = queries.shape
    heads = log_norm.shape[0]
    width = keys.shape[1]
    team = lax.axis_size("team")
    spot = lax.axis_index("team")
    place = lax.axis_index("blk") * team + spot
    begin = (doc_start - place * rows).reshape(1, rows)
    mine = jnp.concatenate([keys.T, values.T], 0)
    own = jnp.concatenate([mine] + [exchanged(mine, "team", k) for k in range(1, team)], 1)
    near = around(own, "blk", 1)

    def shape(*dims, dtype=jnp.float32):
        return pltpu.VMEM(dims, dtype)

    slab = shape(2 * width, rows)
    pieces = [shape(2 * width, rows, dtype=jnp.bfloat16)] * (team - 1)
    acc = pltpu.VMEM((team * rows, 2 * width), jnp.float32)
    part, delta, own_self, *own_pieces = pl.pallas_call(
        own_body,
        out_shape=[shape(features, rows), shape(heads, rows), slab] + pieces,
        in_specs=in_vmem(6),
        out_specs=in_vmem(2 + team),
        scratch_shapes=[acc],
    )(*held(queries, out_grad, attn_out, log_norm, begin, own))

    def body(*refs):
        near_body(team, *refs)

    query_grad, near_self, *sent = pl.pallas_call(
        body,
        out_shape=[shape(rows, features, dtype=jnp.bfloat16), slab] + pieces,
        in_specs=in_vmem(6 + team),
        out_specs=in_vmem(1 + team),
        scratch_shapes=[acc],
    )(*held(queries, out_grad, log_norm, begin, near, part, delta, *own_pieces))
    got = [exchanged(sent[k - 1], "team", k).astype(jnp.float32) for k in range(1, team)]
    nothing = jnp.float32(0.0)
    near_sum, own_sum = near_self, own_self
    for step in range(1, team):
        later = (spot ^ step) > spot
        near_sum = near_sum + jnp.where(later, nothing, got[step - 1])
        own_sum = own_sum + jnp.where(later, got[step - 1], nothing)
    back = around(near_sum.astype(jnp.bfloat16), "blk", -1)
    total = (own_sum + back.astype(jnp.float32)).astype(jnp.bfloat16)
    return (query_grad, total[:width].T, total[width:].T)


def solution(mesh):
    row = P(("blk", "team"), None)
    return jax.shard_map(
        per_device,
        mesh=mesh,
        in_specs=(row, row, row, row, row, P(None, ("blk", "team")), P(("blk", "team"))),
        out_specs=(row, row, row),
        check_vma=False,
    )
```

```python
import functools
import math

import jax
import jax.numpy as jnp
from jax import lax
from jax.experimental import pallas as pl
from jax.experimental.pallas import tpu as pltpu
from jax.sharding import PartitionSpec as P


NT = (((1,), (1,)), ((), ()))
NN = (((1,), (0,)), ((), ()))
FRONT = 6


def around(x, axis, by):
    count = lax.axis_size(axis)
    return lax.ppermute(x, axis, [(i, (i + by) % count) for i in range(count)])


def exchanged(x, axis, step):
    count = lax.axis_size(axis)
    return lax.ppermute(x, axis, [(i, i ^ step) for i in range(count)])


def dot(a, b, dims):
    return lax.dot_general(a, b, dims, preferred_element_type=jnp.float32)


def half_turn(x, width):
    return jnp.concatenate([x[:, width:], x[:, :width]], 1)


def front_body(
    q_in, g_in, o_ref, log_in, begin_in, q_ref, g_ref, stack_ref, delta_ref, log_ref, begin_ref
):
    rows, features = q_in.shape
    heads = log_in.shape[0]
    width = features // heads
    lanes = 2 * width
    q_ref[...] = q_in[...]
    g_ref[...] = g_in[...]
    log_ref[...] = log_in[...]
    place = lax.axis_index("blk") * lax.axis_size("team") + lax.axis_index("team")
    begin_ref[...] = begin_in[...] - place * rows
    prod = g_in[...].astype(jnp.float32) * o_ref[...].astype(jnp.float32)
    feature = lax.broadcasted_iota(jnp.int32, (heads, features), 1)
    head_of = lax.broadcasted_iota(jnp.int32, (heads, features), 0)
    pick = (feature // width == head_of).astype(jnp.float32)
    delta_ref[...] = lax.dot_general(
        pick, prod, NT, precision=lax.Precision.HIGHEST, preferred_element_type=jnp.float32
    )
    row_low = lax.broadcasted_iota(jnp.int32, (rows, lanes), 1) < width
    for pair in range(heads // 2):
        span = slice(pair * lanes, (pair + 1) * lanes)
        q_pair = q_in[:, span]
        g_pair = g_in[:, span]
        blank = jnp.zeros_like(q_pair)
        parts = (
            jnp.where(row_low, q_pair, blank),
            jnp.where(row_low, half_turn(q_pair, width), blank),
            jnp.where(row_low, blank, half_turn(g_pair, width)),
            jnp.where(row_low, blank, g_pair),
        )
        for n, part in enumerate(parts):
            at = (4 * pair + n) * rows
            stack_ref[at : at + rows, :] = part


def tile_terms(slab_refs, bases, front, grad_ref, acc_ref):
    q_ref, g_ref, stack_ref, delta_ref, log_ref, begin_ref = front
    lanes = slab_refs[0].shape[0]
    width = lanes // 2
    rows = q_ref.shape[0]
    total = len(slab_refs) * rows
    heads = log_ref.shape[0]
    kv = jnp.concatenate([ref[...] for ref in slab_refs], 1).T
    low_key = lax.broadcasted_iota(jnp.int32, (total, lanes), 1) < width
    none = jnp.zeros_like(kv)
    k_low = jnp.where(low_key, kv * jnp.asarray(1.0 / math.sqrt(width), kv.dtype), none)
    v_high = jnp.where(low_key, none, kv)
    key_halves = (k_low, half_turn(k_low, width))
    value_halves = (half_turn(v_high, width), v_high)
    inside = lax.broadcasted_iota(jnp.int32, (rows, rows), 0)
    key_pos = jnp.concatenate([inside + base for base in bases], 0)
    row_pos = lax.broadcasted_iota(jnp.int32, (total, rows), 1)
    allowed = (key_pos >= begin_ref[...]) & (key_pos <= row_pos)
    for pair in range(heads // 2):
        span = slice(pair * lanes, (pair + 1) * lanes)
        q_pair = q_ref[:, span]
        g_pair = g_ref[:, span]
        stack = stack_ref[4 * pair * rows : 4 * (pair + 1) * rows, :]
        probs, grads = [], []
        for half in range(2):
            head = 2 * pair + half
            scores = dot(key_halves[half], q_pair, NT)
            shifted = scores - log_ref[head : head + 1, :]
            weights = jnp.exp(jnp.where(allowed, shifted, -jnp.inf))
            prob_grad = dot(value_halves[half], g_pair, NT)
            score_grad = weights * (prob_grad - delta_ref[head : head + 1, :])
            low = score_grad.astype(jnp.bfloat16)
            grad_ref[head * total : (head + 1) * total, :] = low
            probs.append(weights.astype(jnp.bfloat16))
            grads.append(low)
        term = dot(jnp.concatenate(grads + probs, 1), stack, NN)
        if pair == 0:
            acc_ref[...] = term
        else:
            acc_ref[...] += term


def slab_of(acc_ref, step, rows, width):
    part = acc_ref[step * rows : (step + 1) * rows, :].T
    upper = lax.broadcasted_iota(jnp.int32, part.shape, 0) < width
    return part * jnp.where(upper, jnp.float32(1.0 / math.sqrt(width)), jnp.float32(1.0))


def own_body(team, *refs):
    front, slab_refs = refs[:FRONT], refs[FRONT : FRONT + team + 1]
    grad_ref, own_ref, near_ref, *piece_refs, acc_ref = refs[FRONT + team + 1 :]
    rows, features = front[0].shape
    width = features // front[4].shape[0]
    spot = lax.axis_index("team")
    bases = [((spot ^ step) - spot) * rows for step in range(team)] + [-team * rows]
    tile_terms(slab_refs, bases, front, grad_ref, acc_ref)
    own_ref[...] = slab_of(acc_ref, 0, rows, width)
    near_ref[...] = slab_of(acc_ref, team, rows, width)
    for step in range(1, team):
        piece_refs[step - 1][...] = slab_of(acc_ref, step, rows, width).astype(jnp.bfloat16)


def near_body(team, *refs):
    front, slab_refs = refs[:FRONT], refs[FRONT : FRONT + team - 1]
    own_refs = refs[FRONT + team - 1 : FRONT + 2 * team - 2]
    grad_ref, *piece_refs, acc_ref = refs[FRONT + 2 * team - 2 :]
    rows, features = front[0].shape
    width = features // front[4].shape[0]
    spot = lax.axis_index("team")
    has_past = lax.axis_index("blk") > 0

    @pl.when(has_past)
    def _():
        bases = [((spot ^ step) - spot - team) * rows for step in range(1, team)]
        tile_terms(slab_refs, bases, front, grad_ref, acc_ref)
        for step in range(1, team):
            mine = slab_of(acc_ref, step - 1, rows, width).astype(jnp.bfloat16)
            later = jnp.full(mine.shape, (spot ^ step) > spot)
            piece_refs[step - 1][...] = jnp.where(later, mine, own_refs[step - 1][...])

    @pl.when(jnp.logical_not(has_past))
    def _():
        grad_ref[...] = jnp.zeros_like(grad_ref)
        for step in range(1, team):
            kept = own_refs[step - 1][...]
            later = jnp.full(kept.shape, (spot ^ step) > spot)
            piece_refs[step - 1][...] = jnp.where(later, jnp.zeros_like(kept), kept)


def query_body(team, own_grad_ref, near_grad_ref, *refs):
    slab_refs, out_ref = refs[:-1], refs[-1]
    lanes, _ = slab_refs[0].shape
    width = lanes // 2
    heads = out_ref.shape[1] // width
    small = jnp.asarray(1.0 / math.sqrt(width), slab_refs[0].dtype)
    own_keys = jnp.concatenate([ref[:width, :] for ref in slab_refs[: team + 1]], 1) * small
    near_keys = jnp.concatenate([ref[:width, :] for ref in slab_refs[team + 1 :]], 1) * small

    def flipped(head):
        terms = 0.0
        for keys, grads in ((own_keys, own_grad_ref), (near_keys, near_grad_ref)):
            total = keys.shape[1]
            terms += dot(keys, grads[head * total : (head + 1) * total, :], NN)
        return terms

    for pair in range(heads // 2):
        both = jnp.concatenate([flipped(2 * pair), flipped(2 * pair + 1)], 0)
        out_ref[:, pair * lanes : (pair + 1) * lanes] = both.T.astype(out_ref.dtype)


def in_vmem(count):
    return [pl.BlockSpec(memory_space=pltpu.VMEM) for _ in range(count)]


def held(*arrays, space=pltpu.VMEM):
    return [pltpu.with_memory_space_constraint(x, space) for x in arrays]


def grant(slabs, rows, lanes):
    return pltpu.CompilerParams(vmem_limit_bytes=(8 << 20) + 96 * slabs * rows * lanes)


def per_device(queries, keys, values, attn_out, out_grad, log_norm, doc_start):
    rows, features = queries.shape
    heads = log_norm.shape[0]
    width = keys.shape[1]
    team = lax.axis_size("team")
    spot = lax.axis_index("team")
    mine = jnp.concatenate([keys.T, values.T], 0)
    past = around(mine, "blk", 1)
    own = [exchanged(mine, "team", k) for k in range(1, team)]
    near = [exchanged(past, "team", k) for k in range(1, team)]

    def low(*dims):
        return pltpu.VMEM(dims, jnp.bfloat16)

    def full(*dims):
        return pltpu.VMEM(dims, jnp.float32)

    pieces = [low(2 * width, rows)] * (team - 1)
    slab = full(2 * width, rows)
    params = grant(team + 1, rows, 2 * width)
    front = pl.pallas_call(
        front_body,
        out_shape=[
            low(rows, features),
            low(rows, features),
            low(2 * heads * rows, 2 * width),
            full(heads, rows),
            full(heads, rows),
            pltpu.VMEM((1, rows), jnp.int32),
        ],
        in_specs=in_vmem(5),
        out_specs=in_vmem(FRONT),
        compiler_params=params,
    )(*held(queries, out_grad, attn_out, log_norm, doc_start.reshape(1, rows), space=pltpu.HBM))
    own_grads, own_sum, near_sum, *own_pieces = pl.pallas_call(
        functools.partial(own_body, team),
        out_shape=[low(heads * (team + 1) * rows, rows), slab, slab] + pieces,
        in_specs=in_vmem(FRONT + team + 1),
        out_specs=in_vmem(2 + team),
        compiler_params=params,
        scratch_shapes=[full((team + 1) * rows, 2 * width)],
    )(*held(*front, mine, *own, past))
    near_grads, *sent = pl.pallas_call(
        functools.partial(near_body, team),
        out_shape=[low(heads * (team - 1) * rows, rows)] + pieces,
        in_specs=in_vmem(FRONT + 2 * team - 2),
        out_specs=in_vmem(team),
        compiler_params=params,
        scratch_shapes=[full((team - 1) * rows, 2 * width)],
    )(*held(*front, *near, *own_pieces))
    query_grad = pl.pallas_call(
        functools.partial(query_body, team),
        out_shape=jax.ShapeDtypeStruct((rows, features), jnp.bfloat16),
        in_specs=in_vmem(2 + 2 * team),
        out_specs=in_vmem(1)[0],
        compiler_params=params,
    )(*held(own_grads, near_grads, mine, *own, past, *near))
    got = [exchanged(sent[k - 1], "team", k).astype(jnp.float32) for k in range(1, team)]
    nothing = jnp.float32(0.0)
    for step in range(1, team):
        later = (spot ^ step) > spot
        near_sum = near_sum + jnp.where(later, nothing, got[step - 1])
        own_sum = own_sum + jnp.where(later, got[step - 1], nothing)
    back = around(near_sum.astype(jnp.bfloat16), "blk", -1)
    total = (own_sum + back.astype(jnp.float32)).astype(jnp.bfloat16)
    return (query_grad, total[:width].T, total[width:].T)


def solution(mesh):
    row = P(("blk", "team"), None)

    return jax.shard_map(
        per_device,
        mesh=mesh,
        in_specs=(row, row, row, row, row, P(None, ("blk", "team")), P(("blk", "team"))),
        out_specs=(row, row, row),
        check_vma=False,
    )
```

```python
import functools
import math

import jax
import jax.numpy as jnp
from jax import lax
from jax.experimental import pallas as pl
from jax.experimental.pallas import tpu as pltpu
from jax.sharding import PartitionSpec as P


NT = (((1,), (1,)), ((), ()))
NN = (((1,), (0,)), ((), ()))
FRONT = 4


def around(x, axis, by):
    count = lax.axis_size(axis)
    return lax.ppermute(x, axis, [(i, (i + by) % count) for i in range(count)])


def exchanged(x, axis, step):
    count = lax.axis_size(axis)
    return lax.ppermute(x, axis, [(i, i ^ step) for i in range(count)])


def dot(a, b, dims):
    return lax.dot_general(a, b, dims, preferred_element_type=jnp.float32)


def half_turn(x, width):
    return jnp.concatenate([x[:, width:], x[:, :width]], 1)


def front_body(q_in, g_in, o_ref, log_in, begin_in, rows_ref, aux_ref):
    rows, features = q_in.shape
    heads = log_in.shape[0]
    width = features // heads
    rows_ref[:, :features] = q_in[...]
    rows_ref[:, features:] = g_in[...]
    aux_ref[:heads, :] = log_in[...]
    prod = g_in[...].astype(jnp.float32) * o_ref[...].astype(jnp.float32)
    feature = lax.broadcasted_iota(jnp.int32, (heads, features), 1)
    head_of = lax.broadcasted_iota(jnp.int32, (heads, features), 0)
    pick = (feature // width == head_of).astype(jnp.float32)
    aux_ref[heads : 2 * heads, :] = lax.dot_general(
        pick, prod, NT, precision=lax.Precision.HIGHEST, preferred_element_type=jnp.float32
    )
    begin = begin_in[...].astype(jnp.float32)
    aux_ref[2 * heads :, :] = jnp.broadcast_to(begin, (heads, rows))


def tile_terms(slab_refs, bases, front, grad_ref, key_acc, value_acc):
    mine_ref, other_ref, aux_ref, aux_other_ref = front
    lanes, rows = slab_refs[0].shape
    width = lanes // 2
    heads = aux_ref.shape[0] // 3
    features = heads * width
    total = len(slab_refs) * rows
    spot = lax.axis_index("team")
    first_row = (lax.axis_index("blk") * lax.axis_size("team") + spot) * rows

    def of_rows(index):
        at = slice(index, index + 1)
        return jnp.concatenate([aux_ref[at, :], aux_other_ref[at, :]], 1)

    def pair_rows(start):
        span = slice(start, start + lanes)
        return jnp.concatenate([mine_ref[:, span], other_ref[:, span]], 0)

    kv = jnp.concatenate([ref[...] for ref in slab_refs], 1).T
    low_key = lax.broadcasted_iota(jnp.int32, (total, lanes), 1) < width
    none = jnp.zeros_like(kv)
    k_low = jnp.where(low_key, kv * jnp.asarray(1.0 / math.sqrt(width), kv.dtype), none)
    v_high = jnp.where(low_key, none, kv)
    key_halves = (k_low, half_turn(k_low, width))
    value_halves = (half_turn(v_high, width), v_high)
    inside = lax.broadcasted_iota(jnp.int32, (rows, 2 * rows), 0)
    key_pos = jnp.concatenate([inside + base for base in bases], 0)
    lane = lax.broadcasted_iota(jnp.int32, (1, 2 * rows), 1)
    row_pos = jnp.where(lane < rows, lane, lane + ((spot ^ 1) - spot - 1) * rows)
    begin = of_rows(2 * heads).astype(jnp.int32) - first_row
    allowed = (key_pos >= begin) & (key_pos <= row_pos)
    low_row = lax.broadcasted_iota(jnp.int32, (2 * rows, lanes), 1) < width
    for pair in range(heads // 2):
        q_pair = pair_rows(pair * lanes)
        g_pair = pair_rows(features + pair * lanes)
        blank = jnp.zeros_like(q_pair)
        probs, grads = [], []
        for half in range(2):
            head = 2 * pair + half
            scores = dot(key_halves[half], q_pair, NT)
            shifted = scores - of_rows(head)
            weights = jnp.exp(jnp.where(allowed, shifted, -jnp.inf))
            prob_grad = dot(value_halves[half], g_pair, NT)
            score_grad = weights * (prob_grad - of_rows(heads + head))
            low = score_grad.astype(jnp.bfloat16)
            grad_ref[head * total : (head + 1) * total, :] = low
            probs.append(weights.astype(jnp.bfloat16))
            grads.append(low)
        for acc, left, right in ((key_acc, grads, q_pair), (value_acc, probs, g_pair)):
            parts = [jnp.where(low_row, right, blank), jnp.where(low_row, blank, right)]
            term = dot(jnp.concatenate(left, 1), jnp.concatenate(parts, 0), NN)
            if pair == 0:
                acc[...] = term
            else:
                acc[...] += term


def slab_of(key_acc, value_acc, number, rows, width):
    keys = key_acc[number * rows : (number + 1) * rows, :]
    values = value_acc[number * rows : (number + 1) * rows, :]
    keys = (keys + half_turn(keys, width)) * jnp.float32(1.0 / math.sqrt(width))
    values = values + half_turn(values, width)
    low = lax.broadcasted_iota(jnp.int32, keys.shape, 1) < width
    return jnp.where(low, keys, values).T


def own_body(*refs):
    front, slab_refs = refs[:FRONT], refs[FRONT : FRONT + 2]
    grad_ref, own_ref, near_ref, key_acc, value_acc = refs[FRONT + 2 :]
    lanes, rows = slab_refs[0].shape
    bases = [0, -lax.axis_size("team") * rows]
    tile_terms(slab_refs, bases, front, grad_ref, key_acc, value_acc)
    own_ref[...] = slab_of(key_acc, value_acc, 0, rows, lanes // 2)
    near_ref[...] = slab_of(key_acc, value_acc, 1, rows, lanes // 2)


def rest_body(steps, *refs):
    count = len(steps)
    front, slab_refs = refs[:FRONT], refs[FRONT : FRONT + count]
    grad_ref, *piece_refs, key_acc, value_acc = refs[FRONT + count :]
    lanes, rows = slab_refs[0].shape
    spot = lax.axis_index("team")
    block = lax.axis_size("team")
    bases = []
    for step in steps:
        slot = spot ^ step
        bases.append((slot - spot - jnp.where(slot > spot, block, 0)) * rows)
    tile_terms(slab_refs, bases, front, grad_ref, key_acc, value_acc)
    for n, piece_ref in enumerate(piece_refs):
        part = slab_of(key_acc, value_acc, n, rows, lanes // 2)
        piece_ref[...] = part.astype(jnp.bfloat16)


def query_body(own_grad_ref, near_grad_ref, *refs):
    slab_refs, (mine_ref, other_ref) = refs[:-2], refs[-2:]
    lanes, rows = slab_refs[0].shape
    width = lanes // 2
    heads = mine_ref.shape[1] // width
    small = jnp.asarray(1.0 / math.sqrt(width), slab_refs[0].dtype)
    own_keys = jnp.concatenate([ref[:width, :] for ref in slab_refs[:2]], 1) * small
    near_keys = jnp.concatenate([ref[:width, :] for ref in slab_refs[2:]], 1) * small

    def flipped(head):
        terms = 0.0
        for keys, grads in ((own_keys, own_grad_ref), (near_keys, near_grad_ref)):
            total = keys.shape[1]
            terms += dot(keys, grads[head * total : (head + 1) * total, :], NN)
        return terms

    for pair in range(heads // 2):
        both = jnp.concatenate([flipped(2 * pair), flipped(2 * pair + 1)], 0)
        span = slice(pair * lanes, (pair + 1) * lanes)
        mine_ref[:, span] = both[:, :rows].T
        other_ref[:, span] = both[:, rows:].T.astype(jnp.bfloat16)


def in_vmem(count):
    return [pl.BlockSpec(memory_space=pltpu.VMEM) for _ in range(count)]


def held(*arrays, space=pltpu.VMEM):
    return [pltpu.with_memory_space_constraint(x, space) for x in arrays]


def grant(slabs, rows, lanes):
    return pltpu.CompilerParams(vmem_limit_bytes=(8 << 20) + 192 * slabs * rows * lanes)


def per_device(queries, keys, values, attn_out, out_grad, log_norm, doc_start):
    rows, features = queries.shape
    heads = log_norm.shape[0]
    width = keys.shape[1]
    lanes = 2 * width
    half = lax.axis_size("team") // 2
    spot = lax.axis_index("team")
    steps = [2 * n for n in range(1, half)]

    def low(*dims):
        return pltpu.VMEM(dims, jnp.bfloat16)

    def full(*dims):
        return pltpu.VMEM(dims, jnp.float32)

    slab = full(lanes, rows)
    params = grant(max(2, half), rows, lanes)
    mine = jnp.concatenate([keys.T, values.T], 0)
    past = around(mine, "blk", 1)
    own_rows, aux = pl.pallas_call(
        front_body,
        out_shape=[low(rows, 2 * features), full(3 * heads, rows)],
        in_specs=in_vmem(5),
        out_specs=in_vmem(2),
        compiler_params=params,
    )(
        *held(
            queries,
            out_grad,
            attn_out,
            log_norm,
            doc_start.reshape(1, rows),
            space=pltpu.HBM,
        )
    )
    other_rows = exchanged(own_rows, "team", 1)
    other_aux = exchanged(aux, "team", 1)
    front = (own_rows, other_rows, aux, other_aux)
    seen = []
    for k in steps:
        chosen = jnp.where((spot ^ k) < spot, past, mine)
        seen.append(exchanged(chosen, "team", k))
    own_grads, own_sum, near_sum = pl.pallas_call(
        own_body,
        out_shape=[low(2 * heads * rows, 2 * rows), slab, slab],
        in_specs=in_vmem(FRONT + 2),
        out_specs=in_vmem(3),
        scratch_shapes=[full(2 * rows, lanes)] * 2,
        compiler_params=params,
    )(*held(*front, mine, past))
    rest_grads, *sent = pl.pallas_call(
        functools.partial(rest_body, steps),
        out_shape=[low(heads * (half - 1) * rows, 2 * rows)] + [low(lanes, rows)] * (half - 1),
        in_specs=in_vmem(FRONT + half - 1),
        out_specs=in_vmem(half),
        scratch_shapes=[full((half - 1) * rows, lanes)] * 2,
        compiler_params=params,
    )(*held(*front, *seen))
    query_mine, query_other = pl.pallas_call(
        query_body,
        out_shape=[full(rows, features), low(rows, features)],
        in_specs=in_vmem(3 + half),
        out_specs=in_vmem(2),
        compiler_params=params,
    )(*held(own_grads, rest_grads, mine, past, *seen))
    query_back = exchanged(query_other, "team", 1)
    query_grad = (query_mine + query_back.astype(jnp.float32)).astype(jnp.bfloat16)
    nothing = jnp.float32(0.0)
    for k, piece in zip(steps, sent):
        got = exchanged(piece, "team", k).astype(jnp.float32)
        later = (spot ^ k) > spot
        near_sum = near_sum + jnp.where(later, nothing, got)
        own_sum = own_sum + jnp.where(later, got, nothing)
    back = around(near_sum.astype(jnp.bfloat16), "blk", -1)
    total = (own_sum + back.astype(jnp.float32)).astype(jnp.bfloat16)
    return (query_grad, total[:width].T, total[width:].T)


def solution(mesh):
    row = P(("blk", "team"), None)

    return jax.shard_map(
        per_device,
        mesh=mesh,
        in_specs=(row, row, row, row, row, P(None, ("blk", "team")), P(("blk", "team"))),
        out_specs=(row, row, row),
        check_vma=False,
    )
```

```python
import functools
import math

import jax
import jax.numpy as jnp
from jax import lax
from jax.experimental import pallas as pl
from jax.experimental.pallas import tpu as pltpu
from jax.sharding import PartitionSpec as P


NT = (((1,), (1,)), ((), ()))
NN = (((1,), (0,)), ((), ()))
FRONT = 4


def around(x, axis, by):
    count = lax.axis_size(axis)
    pairs = [(i, (i + by) % count) for i in range(count) if by > 0 or i + by >= 0]
    return lax.ppermute(x, axis, pairs)


def exchanged(x, axis, step):
    count = lax.axis_size(axis)
    return lax.ppermute(x, axis, [(i, i ^ step) for i in range(count)])


def sent_home(x, step):
    team, blk = lax.axis_size("team"), lax.axis_size("blk")
    pairs = []
    for t in range(team):
        slot = t ^ step
        for b in range(blk):
            home = b - 1 if slot > t else b
            if home >= 0:
                pairs.append((t * blk + b, slot * blk + home))
    return lax.ppermute(x, ("team", "blk"), pairs)


def dot(a, b, dims):
    return lax.dot_general(a, b, dims, preferred_element_type=jnp.float32)


def half_turn(x, width):
    return jnp.concatenate([x[:, width:], x[:, :width]], 1)


def front_body(q_in, g_in, o_ref, log_in, begin_in, rows_ref, aux_ref):
    rows, features = q_in.shape
    heads = log_in.shape[0]
    width = features // heads
    rows_ref[:, :features] = q_in[...]
    rows_ref[:, features:] = g_in[...]
    aux_ref[:heads, :] = log_in[...]
    prod = g_in[...].astype(jnp.float32) * o_ref[...].astype(jnp.float32)
    feature = lax.broadcasted_iota(jnp.int32, (heads, features), 1)
    head_of = lax.broadcasted_iota(jnp.int32, (heads, features), 0)
    pick = (feature // width == head_of).astype(jnp.float32)
    aux_ref[heads : 2 * heads, :] = lax.dot_general(
        pick, prod, NT, precision=lax.Precision.HIGHEST, preferred_element_type=jnp.float32
    )
    begin = begin_in[...].astype(jnp.float32)
    aux_ref[2 * heads :, :] = jnp.broadcast_to(begin, (heads, rows))


def tile_terms(slab_refs, bases, front, grad_ref, key_acc, value_acc):
    mine_ref, other_ref, aux_ref, aux_other_ref = front
    lanes, rows = slab_refs[0].shape
    width = lanes // 2
    heads = aux_ref.shape[0] // 3
    features = heads * width
    total = len(slab_refs) * rows
    stride = grad_ref.shape[0] // heads
    spot = lax.axis_index("team")
    first_row = (lax.axis_index("blk") * lax.axis_size("team") + spot) * rows

    def of_rows(index):
        at = slice(index, index + 1)
        return jnp.concatenate([aux_ref[at, :], aux_other_ref[at, :]], 1)

    def pair_rows(start):
        span = slice(start, start + lanes)
        return jnp.concatenate([mine_ref[:, span], other_ref[:, span]], 0)

    kv = jnp.concatenate([ref[...] for ref in slab_refs], 1).T
    low_key = lax.broadcasted_iota(jnp.int32, (total, lanes), 1) < width
    none = jnp.zeros_like(kv)
    k_low = jnp.where(low_key, kv * jnp.asarray(1.0 / math.sqrt(width), kv.dtype), none)
    v_high = jnp.where(low_key, none, kv)
    key_halves = (k_low, half_turn(k_low, width))
    value_halves = (half_turn(v_high, width), v_high)
    inside = lax.broadcasted_iota(jnp.int32, (rows, 2 * rows), 0)
    key_pos = jnp.concatenate([inside + base for base in bases], 0)
    lane = lax.broadcasted_iota(jnp.int32, (1, 2 * rows), 1)
    row_pos = jnp.where(lane < rows, lane, lane + ((spot ^ 1) - spot - 1) * rows)
    begin = of_rows(2 * heads).astype(jnp.int32) - first_row
    allowed = (key_pos >= begin) & (key_pos <= row_pos)
    low_row = lax.broadcasted_iota(jnp.int32, (2 * rows, lanes), 1) < width
    for pair in range(heads // 2):
        q_pair = pair_rows(pair * lanes)
        g_pair = pair_rows(features + pair * lanes)
        blank = jnp.zeros_like(q_pair)
        probs, grads = [], []
        for half in range(2):
            head = 2 * pair + half
            scores = dot(key_halves[half], q_pair, NT)
            shifted = scores - of_rows(head)
            weights = jnp.exp(jnp.where(allowed, shifted, -jnp.inf))
            prob_grad = dot(value_halves[half], g_pair, NT)
            score_grad = weights * (prob_grad - of_rows(heads + head))
            low = score_grad.astype(jnp.bfloat16)
            grad_ref[head * stride : head * stride + total, :] = low
            probs.append(weights.astype(jnp.bfloat16))
            grads.append(low)
        for acc, left, right in ((key_acc, grads, q_pair), (value_acc, probs, g_pair)):
            parts = [jnp.where(low_row, right, blank), jnp.where(low_row, blank, right)]
            term = dot(jnp.concatenate(left, 1), jnp.concatenate(parts, 0), NN)
            if pair == 0:
                acc[:total, :] = term
            else:
                acc[:total, :] += term


def slab_of(key_acc, value_acc, number, rows, width):
    keys = key_acc[number * rows : (number + 1) * rows, :]
    values = value_acc[number * rows : (number + 1) * rows, :]
    keys = (keys + half_turn(keys, width)) * jnp.float32(1.0 / math.sqrt(width))
    values = values + half_turn(values, width)
    low = lax.broadcasted_iota(jnp.int32, keys.shape, 1) < width
    return jnp.where(low, keys, values).T


def own_body(*refs):
    front, slab_refs = refs[:FRONT], refs[FRONT : FRONT + 2]
    grad_ref, own_ref, near_ref, key_acc, value_acc = refs[FRONT + 2 :]
    lanes, rows = slab_refs[0].shape
    heads = grad_ref.shape[0] // (2 * rows)
    has_past = lax.axis_index("blk") > 0

    @pl.when(has_past)
    def _():
        bases = [0, -lax.axis_size("team") * rows]
        tile_terms(slab_refs, bases, front, grad_ref, key_acc, value_acc)
        part = slab_of(key_acc, value_acc, 1, rows, lanes // 2)
        near_ref[...] = part.astype(jnp.bfloat16)

    @pl.when(jnp.logical_not(has_past))
    def _():
        tile_terms(slab_refs[:1], [0], front, grad_ref, key_acc, value_acc)
        near_ref[...] = jnp.zeros_like(near_ref)
        for head in range(heads):
            at = (2 * head + 1) * rows
            grad_ref[at : at + rows, :] = jnp.zeros((rows, 2 * rows), grad_ref.dtype)

    own_ref[...] = slab_of(key_acc, value_acc, 0, rows, lanes // 2)


def rest_body(steps, *refs):
    count = len(steps)
    front, slab_refs = refs[:FRONT], refs[FRONT : FRONT + count]
    grad_ref, *piece_refs, key_acc, value_acc = refs[FRONT + count :]
    lanes, rows = slab_refs[0].shape
    spot = lax.axis_index("team")
    block = lax.axis_size("team")
    bases = []
    for step in steps:
        slot = spot ^ step
        bases.append((slot - spot - jnp.where(slot > spot, block, 0)) * rows)
    tile_terms(slab_refs, bases, front, grad_ref, key_acc, value_acc)
    for n, piece_ref in enumerate(piece_refs):
        part = slab_of(key_acc, value_acc, n, rows, lanes // 2)
        piece_ref[...] = part.astype(jnp.bfloat16)


def query_body(own_grad_ref, near_grad_ref, *refs):
    slab_refs, (mine_ref, other_ref) = refs[:-2], refs[-2:]
    lanes, rows = slab_refs[0].shape
    width = lanes // 2
    heads = mine_ref.shape[1] // width
    small = jnp.asarray(1.0 / math.sqrt(width), slab_refs[0].dtype)
    own_keys = jnp.concatenate([ref[:width, :] for ref in slab_refs[:2]], 1) * small
    near_keys = jnp.concatenate([ref[:width, :] for ref in slab_refs[2:]], 1) * small

    def flipped(head):
        terms = 0.0
        for keys, grads in ((own_keys, own_grad_ref), (near_keys, near_grad_ref)):
            total = keys.shape[1]
            terms += dot(keys, grads[head * total : (head + 1) * total, :], NN)
        return terms

    for pair in range(heads // 2):
        both = jnp.concatenate([flipped(2 * pair), flipped(2 * pair + 1)], 0)
        span = slice(pair * lanes, (pair + 1) * lanes)
        mine_ref[:, span] = both[:, :rows].T
        other_ref[:, span] = both[:, rows:].T.astype(jnp.bfloat16)


def in_vmem(count):
    return [pl.BlockSpec(memory_space=pltpu.VMEM) for _ in range(count)]


def held(*arrays, space=pltpu.VMEM):
    return [pltpu.with_memory_space_constraint(x, space) for x in arrays]


def grant(slabs, rows, lanes):
    return pltpu.CompilerParams(vmem_limit_bytes=(8 << 20) + 192 * slabs * rows * lanes)


def per_device(queries, keys, values, attn_out, out_grad, log_norm, doc_start):
    rows, features = queries.shape
    heads = log_norm.shape[0]
    width = keys.shape[1]
    lanes = 2 * width
    half = lax.axis_size("team") // 2
    spot = lax.axis_index("team")
    steps = [2 * n for n in range(1, half)]

    def low(*dims):
        return pltpu.VMEM(dims, jnp.bfloat16)

    def full(*dims):
        return pltpu.VMEM(dims, jnp.float32)

    slab = full(lanes, rows)
    params = grant(max(2, half), rows, lanes)
    mine = jnp.concatenate([keys.T, values.T], 0)
    past = around(mine, "blk", 1)
    own_rows, aux = pl.pallas_call(
        front_body,
        out_shape=[low(rows, 2 * features), full(3 * heads, rows)],
        in_specs=in_vmem(5),
        out_specs=in_vmem(2),
        compiler_params=params,
    )(
        *held(
            queries,
            out_grad,
            attn_out,
            log_norm,
            doc_start.reshape(1, rows),
            space=pltpu.HBM,
        )
    )
    other_rows = exchanged(own_rows, "team", 1)
    other_aux = exchanged(aux, "team", 1)
    front = (own_rows, other_rows, aux, other_aux)
    seen = []
    for k in steps:
        chosen = jnp.where((spot ^ k) < spot, past, mine)
        seen.append(exchanged(chosen, "team", k))
    own_grads, total, past_piece = pl.pallas_call(
        own_body,
        out_shape=[low(2 * heads * rows, 2 * rows), slab, low(lanes, rows)],
        in_specs=in_vmem(FRONT + 2),
        out_specs=in_vmem(3),
        scratch_shapes=[full(2 * rows, lanes)] * 2,
        compiler_params=params,
    )(*held(*front, mine, past))
    rest_grads, *sent = pl.pallas_call(
        functools.partial(rest_body, steps),
        out_shape=[low(heads * (half - 1) * rows, 2 * rows)] + [low(lanes, rows)] * (half - 1),
        in_specs=in_vmem(FRONT + half - 1),
        out_specs=in_vmem(half),
        scratch_shapes=[full((half - 1) * rows, lanes)] * 2,
        compiler_params=params,
    )(*held(*front, *seen))
    query_mine, query_other = pl.pallas_call(
        query_body,
        out_shape=[full(rows, features), low(rows, features)],
        in_specs=in_vmem(3 + half),
        out_specs=in_vmem(2),
        compiler_params=params,
    )(*held(own_grads, rest_grads, mine, past, *seen))
    query_back = exchanged(query_other, "team", 1)
    query_grad = (query_mine + query_back.astype(jnp.float32)).astype(jnp.bfloat16)
    got = [around(past_piece, "blk", -1)]
    got += [sent_home(piece, k) for k, piece in zip(steps, sent)]
    for term in got:
        total = total + term.astype(jnp.float32)
    total = total.astype(jnp.bfloat16)
    return (query_grad, total[:width].T, total[width:].T)


def solution(mesh):
    row = P(("blk", "team"), None)

    return jax.shard_map(
        per_device,
        mesh=mesh,
        in_specs=(row, row, row, row, row, P(None, ("blk", "team")), P(("blk", "team"))),
        out_specs=(row, row, row),
        check_vma=False,
    )
```

```python
import functools
import math

import jax
import jax.numpy as jnp
from jax import lax
from jax.experimental import pallas as pl
from jax.experimental.pallas import tpu as pltpu
from jax.sharding import PartitionSpec as P


NT = (((1,), (1,)), ((), ()))
NN = (((1,), (0,)), ((), ()))
FRONT = 2


def around(x, axis, by):
    count = lax.axis_size(axis)
    pairs = [(i, (i + by) % count) for i in range(count) if by > 0 or i + by >= 0]
    return lax.ppermute(x, axis, pairs)


def exchanged(x, axis, step):
    count = lax.axis_size(axis)
    return lax.ppermute(x, axis, [(i, i ^ step) for i in range(count)])


def skewed(x, step, out):
    team, blk = lax.axis_size("team"), lax.axis_size("blk")
    pairs = []
    for t in range(team):
        slot = t ^ step
        for b in range(blk):
            ahead = b + 1 if slot < t else b
            if ahead < blk:
                pairs.append((t * blk + b, slot * blk + ahead))
    if not out:
        pairs = [(there, here) for here, there in pairs]
    return lax.ppermute(x, ("team", "blk"), pairs)


def dot(a, b, dims):
    return lax.dot_general(a, b, dims, preferred_element_type=jnp.float32)


def half_turn(x, width):
    return jnp.concatenate([x[:, width:], x[:, :width]], 1)


def in_parts(x):
    high = x.astype(jnp.bfloat16).astype(jnp.float32)
    middle = (x - high).astype(jnp.bfloat16).astype(jnp.float32)
    return [high, middle, x - high - middle]


def front_body(q_in, g_in, o_ref, log_in, begin_in, k_in, v_in, mine_ref, rows_ref):
    rows, features = q_in.shape
    heads = log_in.shape[0]
    width = features // heads
    lanes = 2 * width
    mine_ref[:width, :] = k_in[...]
    mine_ref[width:, :] = v_in[...]
    for n, ref in enumerate((q_in, g_in)):
        for pair in range(heads // 2):
            at = (n * (heads // 2) + pair) * rows
            rows_ref[at : at + rows, :] = ref[:, pair * lanes : (pair + 1) * lanes]
    prod = g_in[...].astype(jnp.float32) * o_ref[...].astype(jnp.float32)
    feature = lax.broadcasted_iota(jnp.int32, (heads, features), 1)
    head_of = lax.broadcasted_iota(jnp.int32, (heads, features), 0)
    pick = (feature // width == head_of).astype(jnp.float32)
    delta = lax.dot_general(
        pick, prod, NT, precision=lax.Precision.HIGHEST, preferred_element_type=jnp.float32
    )
    begin = jnp.broadcast_to(begin_in[...], (heads, rows))
    begins = [(begin >> 8).astype(jnp.float32), (begin & 255).astype(jnp.float32)]
    parts = in_parts(log_in[...]) + in_parts(delta) + begins
    rows_ref[heads * rows :, :] = jnp.concatenate(parts, 0).astype(jnp.bfloat16)


def tile_terms(slab_refs, bases, front, grad_ref):
    lanes, rows = slab_refs[0].shape
    width = lanes // 2
    heads = front[0].shape[0] // (rows + 8)
    total = len(slab_refs) * rows
    spot = lax.axis_index("team")
    first_row = (lax.axis_index("blk") * lax.axis_size("team") + spot) * rows
    aux = [ref[heads * rows :, :].astype(jnp.float32) for ref in front]

    def of_rows(*parts):
        both = []
        for one in aux:
            both.append(sum(one[part * heads : (part + 1) * heads, :] for part in parts))
        return jnp.concatenate(both, 1)

    def pair_rows(number):
        return jnp.concatenate([ref[number * rows : (number + 1) * rows, :] for ref in front], 0)

    log_norm = of_rows(0, 1, 2)
    delta = of_rows(3, 4, 5)
    begin = of_rows(6)[:1].astype(jnp.int32) * 256 + of_rows(7)[:1].astype(jnp.int32) - first_row
    kv = jnp.concatenate([ref[...] for ref in slab_refs], 1).T
    low_key = lax.broadcasted_iota(jnp.int32, (total, lanes), 1) < width
    none = jnp.zeros_like(kv)
    k_low = jnp.where(low_key, kv * jnp.asarray(1.0 / math.sqrt(width), kv.dtype), none)
    v_high = jnp.where(low_key, none, kv)
    key_halves = (k_low, half_turn(k_low, width))
    value_halves = (half_turn(v_high, width), v_high)
    inside = lax.broadcasted_iota(jnp.int32, (rows, 2 * rows), 0)
    key_pos = jnp.concatenate([inside + base for base in bases], 0)
    lane = lax.broadcasted_iota(jnp.int32, (1, 2 * rows), 1)
    row_pos = jnp.where(lane < rows, lane, lane + ((spot ^ 1) - spot - 1) * rows)
    allowed = (key_pos >= begin) & (key_pos <= row_pos)
    queries, cotangents, probs, grads = [], [], ([], []), ([], [])
    for pair in range(heads // 2):
        q_pair = pair_rows(pair)
        g_pair = pair_rows(heads // 2 + pair)
        queries.append(q_pair)
        cotangents.append(g_pair)
        for half in range(2):
            head = 2 * pair + half
            scores = dot(key_halves[half], q_pair, NT)
            shifted = scores - log_norm[head : head + 1, :]
            weights = jnp.exp(jnp.where(allowed, shifted, -jnp.inf))
            prob_grad = dot(value_halves[half], g_pair, NT)
            score_grad = weights * (prob_grad - delta[head : head + 1, :])
            low = score_grad.astype(jnp.bfloat16)
            grad_ref[head * total : (head + 1) * total, :] = low
            probs[half].append(weights.astype(jnp.bfloat16))
            grads[half].append(low)

    def summed(terms, rights):
        both = jnp.concatenate([jnp.concatenate(terms[half], 1) for half in range(2)], 0)
        both = dot(both, jnp.concatenate(rights, 0), NN)
        return both[:total], both[total:]

    key_even, key_odd = summed(grads, queries)
    value_even, value_odd = summed(probs, cotangents)
    factor = jnp.float32(1.0 / math.sqrt(width))
    low_key = lax.broadcasted_iota(jnp.int32, (total, lanes), 1) < width
    straight = jnp.where(low_key, key_even * factor, value_odd)
    turned = half_turn(jnp.where(low_key, value_even, key_odd * factor), width)
    return straight + turned


def slab_of(terms, number, rows):
    return terms[number * rows : (number + 1) * rows, :].T


def own_body(*refs):
    front, slab_ref, grad_ref, own_ref = refs[:FRONT], refs[FRONT], refs[-2], refs[-1]
    terms = tile_terms([slab_ref], [0], front, grad_ref)
    own_ref[...] = slab_of(terms, 0, slab_ref.shape[1])


def past_body(*refs):
    front, slab_ref, grad_ref, piece_ref = refs[:FRONT], refs[FRONT], refs[-2], refs[-1]
    rows = slab_ref.shape[1]
    has_past = lax.axis_index("blk") > 0

    @pl.when(has_past)
    def _():
        terms = tile_terms([slab_ref], [-lax.axis_size("team") * rows], front, grad_ref)
        piece_ref[...] = slab_of(terms, 0, rows).astype(jnp.bfloat16)

    @pl.when(jnp.logical_not(has_past))
    def _():
        grad_ref[...] = jnp.zeros_like(grad_ref)
        piece_ref[...] = jnp.zeros_like(piece_ref)


def rest_body(steps, *refs):
    count = len(steps)
    front, slab_refs = refs[:FRONT], refs[FRONT : FRONT + count]
    grad_ref, *piece_refs = refs[FRONT + count :]
    _, rows = slab_refs[0].shape
    spot = lax.axis_index("team")
    block = lax.axis_size("team")
    bases = []
    for step in steps:
        slot = spot ^ step
        bases.append((slot - spot - jnp.where(slot > spot, block, 0)) * rows)
    terms = tile_terms(slab_refs, bases, front, grad_ref)
    for n, piece_ref in enumerate(piece_refs):
        part = slab_of(terms, n, rows)
        piece_ref[...] = part.astype(jnp.bfloat16)


def query_body(count, *refs):
    grad_refs, slab_refs, (mine_ref, other_ref) = refs[:3], refs[3 : 3 + count], refs[3 + count :]
    lanes, rows = slab_refs[0].shape
    width = lanes // 2
    heads = mine_ref.shape[1] // width
    small = jnp.asarray(1.0 / math.sqrt(width), slab_refs[0].dtype)
    groups = (slab_refs[:1], slab_refs[1:2], slab_refs[2:])
    keys = [jnp.concatenate([ref[:width, :] for ref in some], 1) * small for some in groups]

    def flipped(head):
        terms = 0.0
        for some, grads in zip(keys, grad_refs):
            total = some.shape[1]
            terms += dot(some, grads[head * total : (head + 1) * total, :], NN)
        return terms

    for pair in range(heads // 2):
        both = jnp.concatenate([flipped(2 * pair), flipped(2 * pair + 1)], 0)
        span = slice(pair * lanes, (pair + 1) * lanes)
        mine_ref[:, span] = both[:, :rows].T
        other_ref[:, span] = both[:, rows:].T.astype(jnp.bfloat16)


def in_vmem(count):
    return [pl.BlockSpec(memory_space=pltpu.VMEM) for _ in range(count)]


def held(*arrays, space=pltpu.VMEM):
    return [pltpu.with_memory_space_constraint(x, space) for x in arrays]


def grant(slabs, rows, lanes):
    return pltpu.CompilerParams(vmem_limit_bytes=(8 << 20) + 192 * slabs * rows * lanes)


def per_device(queries, keys, values, attn_out, out_grad, log_norm, doc_start):
    rows, features = queries.shape
    heads = log_norm.shape[0]
    width = keys.shape[1]
    lanes = 2 * width
    half = lax.axis_size("team") // 2
    steps = [2 * n for n in range(1, half)]

    def low(*dims):
        return pltpu.VMEM(dims, jnp.bfloat16)

    def full(*dims):
        return pltpu.VMEM(dims, jnp.float32)

    params = grant(max(2, half), rows, lanes)
    mine, own_rows = pl.pallas_call(
        front_body,
        out_shape=[low(lanes, rows), low(heads * (rows + 8), lanes)],
        in_specs=in_vmem(7),
        out_specs=in_vmem(2),
        compiler_params=params,
    )(
        *held(
            queries,
            out_grad,
            attn_out,
            log_norm,
            doc_start.reshape(1, rows),
            keys.T,
            values.T,
            space=pltpu.HBM,
        )
    )
    past = around(mine, "blk", 1)
    front = (own_rows, exchanged(own_rows, "team", 1))
    seen = [skewed(mine, k, True) for k in steps]
    own_grads, total = pl.pallas_call(
        own_body,
        out_shape=[low(heads * rows, 2 * rows), full(lanes, rows)],
        in_specs=in_vmem(FRONT + 1),
        out_specs=in_vmem(2),
        compiler_params=params,
    )(*held(*front, mine))
    past_grads, past_piece = pl.pallas_call(
        past_body,
        out_shape=[low(heads * rows, 2 * rows), low(lanes, rows)],
        in_specs=in_vmem(FRONT + 1),
        out_specs=in_vmem(2),
        compiler_params=params,
    )(*held(*front, past))
    rest_grads, *sent = pl.pallas_call(
        functools.partial(rest_body, steps),
        out_shape=[low(heads * (half - 1) * rows, 2 * rows)] + [low(lanes, rows)] * (half - 1),
        in_specs=in_vmem(FRONT + half - 1),
        out_specs=in_vmem(half),
        compiler_params=params,
    )(*held(*front, *seen))
    query_mine, query_other = pl.pallas_call(
        functools.partial(query_body, 1 + half),
        out_shape=[full(rows, features), low(rows, features)],
        in_specs=in_vmem(4 + half),
        out_specs=in_vmem(2),
        compiler_params=params,
    )(*held(own_grads, past_grads, rest_grads, mine, past, *seen))
    query_back = exchanged(query_other, "team", 1)
    query_grad = (query_mine + query_back.astype(jnp.float32)).astype(jnp.bfloat16)
    got = [around(past_piece, "blk", -1)]
    got += [skewed(piece, k, False) for k, piece in zip(steps, sent)]
    for term in got:
        total = total + term.astype(jnp.float32)
    total = total.astype(jnp.bfloat16)
    return (query_grad, total[:width].T, total[width:].T)


def solution(mesh):
    row = P(("blk", "team"), None)

    return jax.shard_map(
        per_device,
        mesh=mesh,
        in_specs=(row, row, row, row, row, P(None, ("blk", "team")), P(("blk", "team"))),
        out_specs=(row, row, row),
        check_vma=False,
    )
```

```python
import functools
import math

import jax
import jax.numpy as jnp
from jax import lax
from jax.experimental import pallas as pl
from jax.experimental.pallas import tpu as pltpu
from jax.sharding import PartitionSpec as P


NT = (((1,), (1,)), ((), ()))
NN = (((1,), (0,)), ((), ()))
FRONT = 2


def around(x, axis, by):
    count = lax.axis_size(axis)
    pairs = [(i, (i + by) % count) for i in range(count) if by > 0 or i + by >= 0]
    return lax.ppermute(x, axis, pairs)


def exchanged(x, axis, step):
    count = lax.axis_size(axis)
    return lax.ppermute(x, axis, [(i, i ^ step) for i in range(count)])


def skewed(x, step, out):
    team, blk = lax.axis_size("team"), lax.axis_size("blk")
    pairs = []
    for t in range(team):
        slot = t ^ step
        for b in range(blk):
            ahead = b + 1 if slot < t else b
            if ahead < blk:
                pairs.append((t * blk + b, slot * blk + ahead))
    if not out:
        pairs = [(there, here) for here, there in pairs]
    return lax.ppermute(x, ("team", "blk"), pairs)


def dot(a, b, dims):
    return lax.dot_general(a, b, dims, preferred_element_type=jnp.float32)


def half_turn(x, width):
    return jnp.concatenate([x[:, width:], x[:, :width]], 1)


def in_parts(x):
    high = x.astype(jnp.bfloat16).astype(jnp.float32)
    middle = (x - high).astype(jnp.bfloat16).astype(jnp.float32)
    return [high, middle, x - high - middle]


def load_body(q_in, g_in, o_in, log_in, begin_in, k_in, v_in, *refs):
    mine_ref, rows_ref, o_ref, log_ref, begin_ref, sems = refs
    rows, features = q_in.shape
    width, lanes = k_in.shape[0], rows_ref.shape[1]
    moves = [
        (k_in, mine_ref.at[:width, :]),
        (v_in, mine_ref.at[width:, :]),
        (o_in, o_ref),
        (log_in, log_ref),
        (begin_in, begin_ref),
    ]
    for n, source in enumerate((q_in, g_in)):
        for pair in range(features // lanes):
            at = n * (features // lanes) + pair
            target = rows_ref.at[at * rows : (at + 1) * rows, :]
            moves.append((source.at[:, pair * lanes : (pair + 1) * lanes], target))
    copies = [pltpu.make_async_copy(x, y, sems.at[n]) for n, (x, y) in enumerate(moves)]
    for copy in copies:
        copy.start()
    for copy in copies:
        copy.wait()


def front_body(rows_in, o_ref, log_ref, begin_ref, rows_ref):
    heads, rows = log_ref.shape
    pairs, lanes = heads // 2, rows_in.shape[1]
    width = lanes // 2
    first = pairs * rows
    cotangents = [rows_in[first + n * rows : first + (n + 1) * rows, :] for n in range(pairs)]
    cotangents = jnp.concatenate(cotangents, 1).astype(jnp.float32)
    prod = cotangents * o_ref[...].astype(jnp.float32)
    feature = lax.broadcasted_iota(jnp.int32, (heads, heads * width), 1)
    head_of = lax.broadcasted_iota(jnp.int32, (heads, heads * width), 0)
    pick = (feature // width == head_of).astype(jnp.float32)
    delta = lax.dot_general(
        pick, prod, NT, precision=lax.Precision.HIGHEST, preferred_element_type=jnp.float32
    )
    begin = jnp.broadcast_to(begin_ref[...], (heads, rows))
    begins = [(begin >> 8).astype(jnp.float32), (begin & 255).astype(jnp.float32)]
    parts = in_parts(log_ref[...]) + in_parts(delta) + begins
    rows_ref[heads * rows :, :] = jnp.concatenate(parts, 0).astype(jnp.bfloat16)


def tile_terms(slab_refs, bases, front, grad_ref):
    lanes, rows = slab_refs[0].shape
    width = lanes // 2
    heads = front[0].shape[0] // (rows + 8)
    total = len(slab_refs) * rows
    spot = lax.axis_index("team")
    first_row = (lax.axis_index("blk") * lax.axis_size("team") + spot) * rows
    aux = [ref[heads * rows :, :].astype(jnp.float32) for ref in front]

    def of_rows(*parts):
        both = []
        for one in aux:
            both.append(sum(one[part * heads : (part + 1) * heads, :] for part in parts))
        return jnp.concatenate(both, 1)

    def pair_rows(number):
        return jnp.concatenate([ref[number * rows : (number + 1) * rows, :] for ref in front], 0)

    log_norm = of_rows(0, 1, 2)
    delta = of_rows(3, 4, 5)
    begin = of_rows(6)[:1].astype(jnp.int32) * 256 + of_rows(7)[:1].astype(jnp.int32) - first_row
    kv = jnp.concatenate([ref[...] for ref in slab_refs], 1).T
    low_key = lax.broadcasted_iota(jnp.int32, (total, lanes), 1) < width
    none = jnp.zeros_like(kv)
    k_low = jnp.where(low_key, kv * jnp.asarray(1.0 / math.sqrt(width), kv.dtype), none)
    v_high = jnp.where(low_key, none, kv)
    key_halves = (k_low, half_turn(k_low, width))
    value_halves = (half_turn(v_high, width), v_high)
    inside = lax.broadcasted_iota(jnp.int32, (rows, 2 * rows), 0)
    key_pos = jnp.concatenate([inside + base for base in bases], 0)
    lane = lax.broadcasted_iota(jnp.int32, (1, 2 * rows), 1)
    row_pos = jnp.where(lane < rows, lane, lane + ((spot ^ 1) - spot - 1) * rows)
    allowed = (key_pos >= begin) & (key_pos <= row_pos)
    queries, cotangents, probs, grads = [], [], ([], []), ([], [])
    for pair in range(heads // 2):
        q_pair = pair_rows(pair)
        g_pair = pair_rows(heads // 2 + pair)
        queries.append(q_pair)
        cotangents.append(g_pair)
        for half in range(2):
            head = 2 * pair + half
            scores = dot(key_halves[half], q_pair, NT)
            shifted = scores - log_norm[head : head + 1, :]
            weights = jnp.exp(jnp.where(allowed, shifted, -jnp.inf))
            prob_grad = dot(value_halves[half], g_pair, NT)
            score_grad = weights * (prob_grad - delta[head : head + 1, :])
            low = score_grad.astype(jnp.bfloat16)
            grad_ref[head * total : (head + 1) * total, :] = low
            probs[half].append(weights.astype(jnp.bfloat16))
            grads[half].append(low)

    def summed(terms, rights):
        both = jnp.concatenate([jnp.concatenate(terms[half], 1) for half in range(2)], 0)
        both = dot(both, jnp.concatenate(rights, 0), NN)
        return both[:total], both[total:]

    key_even, key_odd = summed(grads, queries)
    value_even, value_odd = summed(probs, cotangents)
    factor = jnp.float32(1.0 / math.sqrt(width))
    low_key = lax.broadcasted_iota(jnp.int32, (total, lanes), 1) < width
    straight = jnp.where(low_key, key_even * factor, value_odd)
    turned = half_turn(jnp.where(low_key, value_even, key_odd * factor), width)
    return straight + turned


def slab_of(terms, number, rows):
    return terms[number * rows : (number + 1) * rows, :].T


def own_body(*refs):
    front, slab_ref, grad_ref, own_ref = refs[:FRONT], refs[FRONT], refs[-2], refs[-1]
    terms = tile_terms([slab_ref], [0], front, grad_ref)
    own_ref[...] = slab_of(terms, 0, slab_ref.shape[1])


def past_body(*refs):
    front, slab_ref, grad_ref, piece_ref = refs[:FRONT], refs[FRONT], refs[-2], refs[-1]
    rows = slab_ref.shape[1]
    has_past = lax.axis_index("blk") > 0

    @pl.when(has_past)
    def _():
        terms = tile_terms([slab_ref], [-lax.axis_size("team") * rows], front, grad_ref)
        piece_ref[...] = slab_of(terms, 0, rows).astype(jnp.bfloat16)

    @pl.when(jnp.logical_not(has_past))
    def _():
        grad_ref[...] = jnp.zeros_like(grad_ref)
        piece_ref[...] = jnp.zeros_like(piece_ref)


def rest_body(steps, *refs):
    count = len(steps)
    front, slab_refs = refs[:FRONT], refs[FRONT : FRONT + count]
    grad_ref, *piece_refs = refs[FRONT + count :]
    _, rows = slab_refs[0].shape
    spot = lax.axis_index("team")
    block = lax.axis_size("team")
    bases = []
    for step in steps:
        slot = spot ^ step
        bases.append((slot - spot - jnp.where(slot > spot, block, 0)) * rows)
    terms = tile_terms(slab_refs, bases, front, grad_ref)
    for n, piece_ref in enumerate(piece_refs):
        part = slab_of(terms, n, rows)
        piece_ref[...] = part.astype(jnp.bfloat16)


def query_body(count, *refs):
    grad_refs, slab_refs, (mine_ref, other_ref) = refs[:3], refs[3 : 3 + count], refs[3 + count :]
    lanes, rows = slab_refs[0].shape
    width = lanes // 2
    heads = mine_ref.shape[1] // width
    small = jnp.asarray(1.0 / math.sqrt(width), slab_refs[0].dtype)
    groups = (slab_refs[:1], slab_refs[1:2], slab_refs[2:])
    keys = [jnp.concatenate([ref[:width, :] for ref in some], 1) * small for some in groups]

    def flipped(head):
        terms = 0.0
        for some, grads in zip(keys, grad_refs):
            total = some.shape[1]
            terms += dot(some, grads[head * total : (head + 1) * total, :], NN)
        return terms

    for pair in range(heads // 2):
        both = jnp.concatenate([flipped(2 * pair), flipped(2 * pair + 1)], 0)
        span = slice(pair * lanes, (pair + 1) * lanes)
        mine_ref[:, span] = both[:, :rows].T
        other_ref[:, span] = both[:, rows:].T.astype(jnp.bfloat16)


def in_vmem(count):
    return [pl.BlockSpec(memory_space=pltpu.VMEM) for _ in range(count)]


def held(*arrays, space=pltpu.VMEM):
    return [pltpu.with_memory_space_constraint(x, space) for x in arrays]


def grant(slabs, rows, lanes):
    return pltpu.CompilerParams(vmem_limit_bytes=(8 << 20) + 192 * slabs * rows * lanes)


def per_device(queries, keys, values, attn_out, out_grad, log_norm, doc_start):
    rows, features = queries.shape
    heads = log_norm.shape[0]
    width = keys.shape[1]
    lanes = 2 * width
    half = lax.axis_size("team") // 2
    steps = [2 * n for n in range(1, half)]

    def low(*dims):
        return pltpu.VMEM(dims, jnp.bfloat16)

    def full(*dims):
        return pltpu.VMEM(dims, jnp.float32)

    params = grant(max(2, half), rows, lanes)
    mine, loaded, loaded_out, loaded_log, loaded_begin = pl.pallas_call(
        load_body,
        out_shape=[
            low(lanes, rows),
            low(heads * (rows + 8), lanes),
            low(rows, features),
            full(heads, rows),
            pltpu.VMEM((1, rows), jnp.int32),
        ],
        in_specs=[pl.BlockSpec(memory_space=pltpu.HBM)] * 7,
        out_specs=in_vmem(5),
        scratch_shapes=[pltpu.SemaphoreType.DMA((heads + 5,))],
        compiler_params=params,
    )(
        *held(
            queries,
            out_grad,
            attn_out,
            log_norm,
            doc_start.reshape(1, rows),
            keys.T,
            values.T,
            space=pltpu.HBM,
        )
    )
    past = around(mine, "blk", 1)
    own_rows = pl.pallas_call(
        front_body,
        out_shape=low(heads * (rows + 8), lanes),
        in_specs=in_vmem(4),
        out_specs=in_vmem(1)[0],
        input_output_aliases={0: 0},
        compiler_params=params,
    )(*held(loaded, loaded_out, loaded_log, loaded_begin))
    front = (own_rows, exchanged(own_rows, "team", 1))
    seen = [skewed(mine, k, True) for k in steps]
    own_grads, total = pl.pallas_call(
        own_body,
        out_shape=[low(heads * rows, 2 * rows), full(lanes, rows)],
        in_specs=in_vmem(FRONT + 1),
        out_specs=in_vmem(2),
        compiler_params=params,
    )(*held(*front, mine))
    past_grads, past_piece = pl.pallas_call(
        past_body,
        out_shape=[low(heads * rows, 2 * rows), low(lanes, rows)],
        in_specs=in_vmem(FRONT + 1),
        out_specs=in_vmem(2),
        compiler_params=params,
    )(*held(*front, past))
    rest_grads, *sent = pl.pallas_call(
        functools.partial(rest_body, steps),
        out_shape=[low(heads * (half - 1) * rows, 2 * rows)] + [low(lanes, rows)] * (half - 1),
        in_specs=in_vmem(FRONT + half - 1),
        out_specs=in_vmem(half),
        compiler_params=params,
    )(*held(*front, *seen))
    query_mine, query_other = pl.pallas_call(
        functools.partial(query_body, 1 + half),
        out_shape=[full(rows, features), low(rows, features)],
        in_specs=in_vmem(4 + half),
        out_specs=in_vmem(2),
        compiler_params=params,
    )(*held(own_grads, past_grads, rest_grads, mine, past, *seen))
    query_back = exchanged(query_other, "team", 1)
    query_grad = (query_mine + query_back.astype(jnp.float32)).astype(jnp.bfloat16)
    got = [around(past_piece, "blk", -1)]
    got += [skewed(piece, k, False) for k, piece in zip(steps, sent)]
    for term in got:
        total = total + term.astype(jnp.float32)
    total = total.astype(jnp.bfloat16)
    return (query_grad, total[:width].T, total[width:].T)


def solution(mesh):
    row = P(("blk", "team"), None)

    return jax.shard_map(
        per_device,
        mesh=mesh,
        in_specs=(row, row, row, row, row, P(None, ("blk", "team")), P(("blk", "team"))),
        out_specs=(row, row, row),
        check_vma=False,
    )
```

```python
import functools
import math

import jax
import jax.numpy as jnp
from jax import lax
from jax.experimental import pallas as pl
from jax.experimental.pallas import tpu as pltpu
from jax.sharding import PartitionSpec as P


NT = (((1,), (1,)), ((), ()))
NN = (((1,), (0,)), ((), ()))
FRONT = 2


def around(x, axis, by):
    count = lax.axis_size(axis)
    pairs = [(i, (i + by) % count) for i in range(count) if by > 0 or i + by >= 0]
    return lax.ppermute(x, axis, pairs)


def exchanged(x, axis, step):
    count = lax.axis_size(axis)
    return lax.ppermute(x, axis, [(i, i ^ step) for i in range(count)])


def skewed(x, step, out):
    team, blk = lax.axis_size("team"), lax.axis_size("blk")
    pairs = []
    for t in range(team):
        slot = t ^ step
        for b in range(blk):
            ahead = b + 1 if slot < t else b
            if ahead < blk:
                pairs.append((t * blk + b, slot * blk + ahead))
    if not out:
        pairs = [(there, here) for here, there in pairs]
    return lax.ppermute(x, ("team", "blk"), pairs)


def dot(a, b, dims):
    return lax.dot_general(a, b, dims, preferred_element_type=jnp.float32)


def half_turn(x, width):
    return jnp.concatenate([x[:, width:], x[:, :width]], 1)


def in_parts(x):
    high = x.astype(jnp.bfloat16).astype(jnp.float32)
    middle = (x - high).astype(jnp.bfloat16).astype(jnp.float32)
    return [high, middle, x - high - middle]


def load_body(q_in, g_in, o_in, log_in, begin_in, k_in, v_in, *refs):
    mine_ref, rows_ref, o_ref, log_ref, begin_ref, sems = refs
    rows, features = q_in.shape
    width, lanes = k_in.shape[0], rows_ref.shape[1]
    moves = [
        (k_in, mine_ref.at[:width, :]),
        (v_in, mine_ref.at[width:, :]),
        (o_in, o_ref),
        (log_in, log_ref),
        (begin_in, begin_ref),
    ]
    for n, source in enumerate((q_in, g_in)):
        for pair in range(features // lanes):
            at = n * (features // lanes) + pair
            target = rows_ref.at[at * rows : (at + 1) * rows, :]
            moves.append((source.at[:, pair * lanes : (pair + 1) * lanes], target))
    copies = [pltpu.make_async_copy(x, y, sems.at[n]) for n, (x, y) in enumerate(moves)]
    for copy in copies:
        copy.start()
    for copy in copies:
        copy.wait()


def front_body(rows_in, o_ref, log_ref, begin_ref, rows_ref):
    heads, rows = log_ref.shape
    pairs, lanes = heads // 2, rows_in.shape[1]
    width = lanes // 2
    first = pairs * rows
    cotangents = [rows_in[first + n * rows : first + (n + 1) * rows, :] for n in range(pairs)]
    cotangents = jnp.concatenate(cotangents, 1).astype(jnp.float32)
    prod = cotangents * o_ref[...].astype(jnp.float32)
    feature = lax.broadcasted_iota(jnp.int32, (heads, heads * width), 1)
    head_of = lax.broadcasted_iota(jnp.int32, (heads, heads * width), 0)
    pick = (feature // width == head_of).astype(jnp.float32)
    delta = lax.dot_general(
        pick, prod, NT, precision=lax.Precision.HIGHEST, preferred_element_type=jnp.float32
    )
    begin = jnp.broadcast_to(begin_ref[...], (heads, rows))
    begins = [(begin >> 8).astype(jnp.float32), (begin & 255).astype(jnp.float32)]
    parts = in_parts(log_ref[...]) + in_parts(delta) + begins
    rows_ref[heads * rows :, :] = jnp.concatenate(parts, 0).astype(jnp.bfloat16)


def tile_terms(slab_refs, bases, front, grad_ref):
    lanes, rows = slab_refs[0].shape
    width = lanes // 2
    heads = front[0].shape[0] // (rows + 8)
    total = len(slab_refs) * rows
    spot = lax.axis_index("team")
    first_row = (lax.axis_index("blk") * lax.axis_size("team") + spot) * rows
    aux = [ref[heads * rows :, :].astype(jnp.float32) for ref in front]

    def of_rows(*parts):
        both = []
        for one in aux:
            both.append(sum(one[part * heads : (part + 1) * heads, :] for part in parts))
        return jnp.concatenate(both, 1)

    def pair_rows(number):
        return jnp.concatenate([ref[number * rows : (number + 1) * rows, :] for ref in front], 0)

    log_norm = of_rows(0, 1, 2)
    delta = of_rows(3, 4, 5)
    begin = of_rows(6)[:1].astype(jnp.int32) * 256 + of_rows(7)[:1].astype(jnp.int32) - first_row
    kv = jnp.concatenate([ref[...] for ref in slab_refs], 1).T
    low_key = lax.broadcasted_iota(jnp.int32, (total, lanes), 1) < width
    none = jnp.zeros_like(kv)
    k_low = jnp.where(low_key, kv * jnp.asarray(1.0 / math.sqrt(width), kv.dtype), none)
    v_high = jnp.where(low_key, none, kv)
    key_halves = (k_low, half_turn(k_low, width))
    value_halves = (half_turn(v_high, width), v_high)
    inside = lax.broadcasted_iota(jnp.int32, (rows, 2 * rows), 0)
    key_pos = jnp.concatenate([inside + base for base in bases], 0)
    lane = lax.broadcasted_iota(jnp.int32, (1, 2 * rows), 1)
    row_pos = jnp.where(lane < rows, lane, lane + ((spot ^ 1) - spot - 1) * rows)
    allowed = (key_pos >= begin) & (key_pos <= row_pos)
    queries, cotangents, probs, grads = [], [], ([], []), ([], [])
    for pair in range(heads // 2):
        q_pair = pair_rows(pair)
        g_pair = pair_rows(heads // 2 + pair)
        queries.append(q_pair)
        cotangents.append(g_pair)
        for half in range(2):
            head = 2 * pair + half
            scores = dot(key_halves[half], q_pair, NT)
            shifted = scores - log_norm[head : head + 1, :]
            weights = jnp.exp(jnp.where(allowed, shifted, -jnp.inf))
            prob_grad = dot(value_halves[half], g_pair, NT)
            score_grad = weights * (prob_grad - delta[head : head + 1, :])
            low = score_grad.astype(jnp.bfloat16)
            grad_ref[head * total : (head + 1) * total, :] = low
            probs[half].append(weights.astype(jnp.bfloat16))
            grads[half].append(low)

    def summed(terms, rights):
        both = jnp.concatenate([jnp.concatenate(terms[half], 1) for half in range(2)], 0)
        both = dot(both, jnp.concatenate(rights, 0), NN)
        return both[:total], both[total:]

    key_even, key_odd = summed(grads, queries)
    value_even, value_odd = summed(probs, cotangents)
    factor = jnp.float32(1.0 / math.sqrt(width))
    low_key = lax.broadcasted_iota(jnp.int32, (total, lanes), 1) < width
    straight = jnp.where(low_key, key_even * factor, value_odd)
    turned = half_turn(jnp.where(low_key, value_even, key_odd * factor), width)
    return straight + turned


def slab_of(terms, number, rows):
    return terms[number * rows : (number + 1) * rows, :].T


def own_body(*refs):
    front, slab_ref, grad_ref, own_ref = refs[:FRONT], refs[FRONT], refs[-2], refs[-1]
    terms = tile_terms([slab_ref], [0], front, grad_ref)
    own_ref[...] = slab_of(terms, 0, slab_ref.shape[1])


def past_body(*refs):
    front, slab_ref, grad_ref, piece_ref = refs[:FRONT], refs[FRONT], refs[-2], refs[-1]
    rows = slab_ref.shape[1]
    has_past = lax.axis_index("blk") > 0

    @pl.when(has_past)
    def _():
        terms = tile_terms([slab_ref], [-lax.axis_size("team") * rows], front, grad_ref)
        piece_ref[...] = slab_of(terms, 0, rows).astype(jnp.bfloat16)

    @pl.when(jnp.logical_not(has_past))
    def _():
        grad_ref[...] = jnp.zeros_like(grad_ref)
        piece_ref[...] = jnp.zeros_like(piece_ref)


def rest_body(steps, *refs):
    count = len(steps)
    front, slab_refs = refs[:FRONT], refs[FRONT : FRONT + count]
    grad_ref, *piece_refs = refs[FRONT + count :]
    _, rows = slab_refs[0].shape
    spot = lax.axis_index("team")
    block = lax.axis_size("team")
    bases = []
    for step in steps:
        slot = spot ^ step
        bases.append((slot - spot - jnp.where(slot > spot, block, 0)) * rows)
    terms = tile_terms(slab_refs, bases, front, grad_ref)
    for n, piece_ref in enumerate(piece_refs):
        part = slab_of(terms, n, rows)
        piece_ref[...] = part.astype(jnp.bfloat16)


def query_body(count, *refs):
    grad_refs, slab_refs, (mine_ref, other_ref) = refs[:3], refs[3 : 3 + count], refs[3 + count :]
    lanes, rows = slab_refs[0].shape
    width = lanes // 2
    heads = mine_ref.shape[1] // width
    small = jnp.asarray(1.0 / math.sqrt(width), slab_refs[0].dtype)
    groups = (slab_refs[:1], slab_refs[1:2], slab_refs[2:])
    keys = [jnp.concatenate([ref[:width, :] for ref in some], 1) * small for some in groups]

    def flipped(head):
        terms = 0.0
        for some, grads in zip(keys, grad_refs):
            total = some.shape[1]
            terms += dot(some, grads[head * total : (head + 1) * total, :], NN)
        return terms

    for pair in range(heads // 2):
        both = jnp.concatenate([flipped(2 * pair), flipped(2 * pair + 1)], 0)
        span = slice(pair * lanes, (pair + 1) * lanes)
        mine_ref[:, span] = both[:, :rows].T
        other_ref[:, span] = both[:, rows:].T.astype(jnp.bfloat16)


def end_body(query_ref, query_back_ref, total_ref, *refs):
    term_refs, (q_out, k_out, v_out, q_buf, kv_buf, sems) = refs[:-6], refs[-6:]
    width = k_out.shape[0]
    query = query_ref[...] + query_back_ref[...].astype(jnp.float32)
    q_buf[...] = query.astype(q_buf.dtype)
    copies = [pltpu.make_async_copy(q_buf, q_out, sems.at[0])]
    copies[0].start()
    total = total_ref[...]
    for ref in term_refs:
        total = total + ref[...].astype(jnp.float32)
    kv_buf[...] = total.astype(kv_buf.dtype)
    copies.append(pltpu.make_async_copy(kv_buf.at[:width, :], k_out, sems.at[1]))
    copies.append(pltpu.make_async_copy(kv_buf.at[width:, :], v_out, sems.at[2]))
    for copy in copies[1:]:
        copy.start()
    for copy in copies:
        copy.wait()


def in_vmem(count):
    return [pl.BlockSpec(memory_space=pltpu.VMEM) for _ in range(count)]


def held(*arrays, space=pltpu.VMEM):
    return [pltpu.with_memory_space_constraint(x, space) for x in arrays]


def grant(slabs, rows, lanes):
    return pltpu.CompilerParams(vmem_limit_bytes=(8 << 20) + 192 * slabs * rows * lanes)


def per_device(queries, keys, values, attn_out, out_grad, log_norm, doc_start):
    rows, features = queries.shape
    heads = log_norm.shape[0]
    width = keys.shape[1]
    lanes = 2 * width
    half = lax.axis_size("team") // 2
    steps = [2 * n for n in range(1, half)]

    def low(*dims):
        return pltpu.VMEM(dims, jnp.bfloat16)

    def full(*dims):
        return pltpu.VMEM(dims, jnp.float32)

    params = grant(max(2, half), rows, lanes)
    mine, loaded, loaded_out, loaded_log, loaded_begin = pl.pallas_call(
        load_body,
        out_shape=[
            low(lanes, rows),
            low(heads * (rows + 8), lanes),
            low(rows, features),
            full(heads, rows),
            pltpu.VMEM((1, rows), jnp.int32),
        ],
        in_specs=[pl.BlockSpec(memory_space=pltpu.HBM)] * 7,
        out_specs=in_vmem(5),
        scratch_shapes=[pltpu.SemaphoreType.DMA((heads + 5,))],
        compiler_params=params,
    )(
        *held(
            queries,
            out_grad,
            attn_out,
            log_norm,
            doc_start.reshape(1, rows),
            keys.T,
            values.T,
            space=pltpu.HBM,
        )
    )
    past = around(mine, "blk", 1)
    own_rows = pl.pallas_call(
        front_body,
        out_shape=low(heads * (rows + 8), lanes),
        in_specs=in_vmem(4),
        out_specs=in_vmem(1)[0],
        input_output_aliases={0: 0},
        compiler_params=params,
    )(*held(loaded, loaded_out, loaded_log, loaded_begin))
    front = (own_rows, exchanged(own_rows, "team", 1))
    seen = [skewed(mine, k, True) for k in steps]
    own_grads, total = pl.pallas_call(
        own_body,
        out_shape=[low(heads * rows, 2 * rows), full(lanes, rows)],
        in_specs=in_vmem(FRONT + 1),
        out_specs=in_vmem(2),
        compiler_params=params,
    )(*held(*front, mine))
    past_grads, past_piece = pl.pallas_call(
        past_body,
        out_shape=[low(heads * rows, 2 * rows), low(lanes, rows)],
        in_specs=in_vmem(FRONT + 1),
        out_specs=in_vmem(2),
        compiler_params=params,
    )(*held(*front, past))
    rest_grads, *sent = pl.pallas_call(
        functools.partial(rest_body, steps),
        out_shape=[low(heads * (half - 1) * rows, 2 * rows)] + [low(lanes, rows)] * (half - 1),
        in_specs=in_vmem(FRONT + half - 1),
        out_specs=in_vmem(half),
        compiler_params=params,
    )(*held(*front, *seen))
    query_mine, query_other = pl.pallas_call(
        functools.partial(query_body, 1 + half),
        out_shape=[full(rows, features), low(rows, features)],
        in_specs=in_vmem(4 + half),
        out_specs=in_vmem(2),
        compiler_params=params,
    )(*held(own_grads, past_grads, rest_grads, mine, past, *seen))
    query_back = exchanged(query_other, "team", 1)
    got = [around(past_piece, "blk", -1)]
    got += [skewed(piece, k, False) for k, piece in zip(steps, sent)]
    half_grad = jax.ShapeDtypeStruct((width, rows), jnp.bfloat16)
    query_grad, key_grad, value_grad = pl.pallas_call(
        end_body,
        out_shape=[
            jax.ShapeDtypeStruct((rows, features), jnp.bfloat16),
            half_grad,
            half_grad,
        ],
        in_specs=in_vmem(3 + len(got)),
        out_specs=[pl.BlockSpec(memory_space=pltpu.HBM)] * 3,
        scratch_shapes=[
            low(rows, features),
            low(lanes, rows),
            pltpu.SemaphoreType.DMA((3,)),
        ],
        compiler_params=params,
    )(*held(query_mine, query_back, total, *got))
    return (query_grad, key_grad.T, value_grad.T)


def solution(mesh):
    row = P(("blk", "team"), None)

    return jax.shard_map(
        per_device,
        mesh=mesh,
        in_specs=(row, row, row, row, row, P(None, ("blk", "team")), P(("blk", "team"))),
        out_specs=(row, row, row),
        check_vma=False,
    )
```

```python
import functools
import math

import jax
import jax.numpy as jnp
from jax import lax
from jax.experimental import pallas as pl
from jax.experimental.pallas import tpu as pltpu
from jax.sharding import PartitionSpec as P


NT = (((1,), (1,)), ((), ()))
NN = (((1,), (0,)), ((), ()))
FRONT = 2


def around(x, axis, by):
    count = lax.axis_size(axis)
    pairs = [(i, (i + by) % count) for i in range(count) if by > 0 or i + by >= 0]
    return lax.ppermute(x, axis, pairs)


def exchanged(x, axis, step):
    count = lax.axis_size(axis)
    return lax.ppermute(x, axis, [(i, i ^ step) for i in range(count)])


def skewed(x, step, out):
    team, blk = lax.axis_size("team"), lax.axis_size("blk")
    pairs = []
    for t in range(team):
        slot = t ^ step
        for b in range(blk):
            ahead = b + 1 if slot < t else b
            if ahead < blk:
                pairs.append((t * blk + b, slot * blk + ahead))
    if not out:
        pairs = [(there, here) for here, there in pairs]
    return lax.ppermute(x, ("team", "blk"), pairs)


def dot(a, b, dims):
    return lax.dot_general(a, b, dims, preferred_element_type=jnp.float32)


def half_turn(x, width):
    return jnp.concatenate([x[:, width:], x[:, :width]], 1)


def in_parts(x):
    high = x.astype(jnp.bfloat16).astype(jnp.float32)
    middle = (x - high).astype(jnp.bfloat16).astype(jnp.float32)
    return [high, middle, x - high - middle]


def load_body(q_in, g_in, o_in, log_in, begin_in, k_in, v_in, *refs):
    mine_ref, rows_ref, o_ref, log_ref, begin_ref, sems = refs
    rows, features = q_in.shape
    width, lanes = k_in.shape[0], rows_ref.shape[1]
    moves = [
        (k_in, mine_ref.at[:width, :]),
        (v_in, mine_ref.at[width:, :]),
        (o_in, o_ref),
        (log_in, log_ref),
        (begin_in, begin_ref),
    ]
    for n, source in enumerate((q_in, g_in)):
        for pair in range(features // lanes):
            at = n * (features // lanes) + pair
            target = rows_ref.at[at * rows : (at + 1) * rows, :]
            moves.append((source.at[:, pair * lanes : (pair + 1) * lanes], target))
    copies = [pltpu.make_async_copy(x, y, sems.at[n]) for n, (x, y) in enumerate(moves)]
    for copy in copies:
        copy.start()
    for copy in copies:
        copy.wait()


def front_body(rows_in, o_ref, log_ref, begin_ref, rows_ref):
    heads, rows = log_ref.shape
    pairs, lanes = heads // 2, rows_in.shape[1]
    width = lanes // 2
    first = pairs * rows
    cotangents = [rows_in[first + n * rows : first + (n + 1) * rows, :] for n in range(pairs)]
    cotangents = jnp.concatenate(cotangents, 1).astype(jnp.float32)
    prod = cotangents * o_ref[...].astype(jnp.float32)
    feature = lax.broadcasted_iota(jnp.int32, (heads, heads * width), 1)
    head_of = lax.broadcasted_iota(jnp.int32, (heads, heads * width), 0)
    pick = (feature // width == head_of).astype(jnp.float32)
    delta = lax.dot_general(
        pick, prod, NT, precision=lax.Precision.HIGHEST, preferred_element_type=jnp.float32
    )
    begin = jnp.broadcast_to(begin_ref[...], (heads, rows))
    begins = [(begin >> 8).astype(jnp.float32), (begin & 255).astype(jnp.float32)]
    parts = in_parts(log_ref[...]) + in_parts(delta) + begins
    rows_ref[heads * rows :, :] = jnp.concatenate(parts, 0).astype(jnp.bfloat16)


def tile_terms(slab_refs, bases, front, grad_ref):
    lanes, rows = slab_refs[0].shape
    width = lanes // 2
    heads = front[0].shape[0] // (rows + 8)
    total = len(slab_refs) * rows
    spot = lax.axis_index("team")
    first_row = (lax.axis_index("blk") * lax.axis_size("team") + spot) * rows
    aux = [ref[heads * rows :, :].astype(jnp.float32) for ref in front]

    def of_rows(*parts):
        both = []
        for one in aux:
            both.append(sum(one[part * heads : (part + 1) * heads, :] for part in parts))
        return jnp.concatenate(both, 1)

    def pair_rows(number):
        return jnp.concatenate([ref[number * rows : (number + 1) * rows, :] for ref in front], 0)

    log_norm = of_rows(0, 1, 2)
    delta = of_rows(3, 4, 5)
    begin = of_rows(6)[:1].astype(jnp.int32) * 256 + of_rows(7)[:1].astype(jnp.int32) - first_row
    kv = jnp.concatenate([ref[...] for ref in slab_refs], 1).T
    low_key = lax.broadcasted_iota(jnp.int32, (total, lanes), 1) < width
    none = jnp.zeros_like(kv)
    k_low = jnp.where(low_key, kv * jnp.asarray(1.0 / math.sqrt(width), kv.dtype), none)
    v_high = jnp.where(low_key, none, kv)
    key_halves = jnp.concatenate([k_low, half_turn(k_low, width)], 0)
    value_halves = jnp.concatenate([half_turn(v_high, width), v_high], 0)
    inside = lax.broadcasted_iota(jnp.int32, (rows, 2 * rows), 0)
    key_pos = jnp.concatenate([inside + base for base in bases], 0)
    lane = lax.broadcasted_iota(jnp.int32, (1, 2 * rows), 1)
    row_pos = jnp.where(lane < rows, lane, lane + ((spot ^ 1) - spot - 1) * rows)
    allowed = (key_pos >= begin) & (key_pos <= row_pos)
    queries, cotangents, probs, grads = [], [], ([], []), ([], [])
    for pair in range(heads // 2):
        q_pair = pair_rows(pair)
        g_pair = pair_rows(heads // 2 + pair)
        queries.append(q_pair)
        cotangents.append(g_pair)
        scores = dot(key_halves, q_pair, NT)
        prob_grads = dot(value_halves, g_pair, NT)
        for half in range(2):
            span = slice(half * total, (half + 1) * total)
            head = 2 * pair + half
            shifted = scores[span] - log_norm[head : head + 1, :]
            weights = jnp.exp(jnp.where(allowed, shifted, -jnp.inf))
            score_grad = weights * (prob_grads[span] - delta[head : head + 1, :])
            low = score_grad.astype(jnp.bfloat16)
            grad_ref[head * total : (head + 1) * total, :] = low
            probs[half].append(weights.astype(jnp.bfloat16))
            grads[half].append(low)

    def summed(terms, rights):
        both = jnp.concatenate([jnp.concatenate(terms[half], 1) for half in range(2)], 0)
        both = dot(both, jnp.concatenate(rights, 0), NN)
        return both[:total], both[total:]

    key_even, key_odd = summed(grads, queries)
    value_even, value_odd = summed(probs, cotangents)
    factor = jnp.float32(1.0 / math.sqrt(width))
    low_key = lax.broadcasted_iota(jnp.int32, (total, lanes), 1) < width
    straight = jnp.where(low_key, key_even * factor, value_odd)
    turned = half_turn(jnp.where(low_key, value_even, key_odd * factor), width)
    return straight + turned


def slab_of(terms, number, rows):
    return terms[number * rows : (number + 1) * rows, :].T


def own_body(*refs):
    front, slab_ref, grad_ref, own_ref = refs[:FRONT], refs[FRONT], refs[-2], refs[-1]
    terms = tile_terms([slab_ref], [0], front, grad_ref)
    own_ref[...] = slab_of(terms, 0, slab_ref.shape[1])


def past_body(*refs):
    front, slab_ref, grad_ref, piece_ref = refs[:FRONT], refs[FRONT], refs[-2], refs[-1]
    rows = slab_ref.shape[1]
    has_past = lax.axis_index("blk") > 0

    @pl.when(has_past)
    def _():
        terms = tile_terms([slab_ref], [-lax.axis_size("team") * rows], front, grad_ref)
        piece_ref[...] = slab_of(terms, 0, rows).astype(jnp.bfloat16)

    @pl.when(jnp.logical_not(has_past))
    def _():
        grad_ref[...] = jnp.zeros_like(grad_ref)
        piece_ref[...] = jnp.zeros_like(piece_ref)


def rest_body(steps, *refs):
    count = len(steps)
    front, slab_refs = refs[:FRONT], refs[FRONT : FRONT + count]
    grad_ref, *piece_refs = refs[FRONT + count :]
    _, rows = slab_refs[0].shape
    spot = lax.axis_index("team")
    block = lax.axis_size("team")
    bases = []
    for step in steps:
        slot = spot ^ step
        bases.append((slot - spot - jnp.where(slot > spot, block, 0)) * rows)
    terms = tile_terms(slab_refs, bases, front, grad_ref)
    for n, piece_ref in enumerate(piece_refs):
        part = slab_of(terms, n, rows)
        piece_ref[...] = part.astype(jnp.bfloat16)


def query_body(count, *refs):
    grad_refs, slab_refs, (mine_ref, other_ref) = refs[:3], refs[3 : 3 + count], refs[3 + count :]
    lanes, rows = slab_refs[0].shape
    width = lanes // 2
    heads = mine_ref.shape[1] // width
    small = jnp.asarray(1.0 / math.sqrt(width), slab_refs[0].dtype)
    groups = (slab_refs[:1], slab_refs[1:2], slab_refs[2:])
    keys = [jnp.concatenate([ref[:width, :] for ref in some], 1) * small for some in groups]

    def flipped(head):
        terms = 0.0
        for some, grads in zip(keys, grad_refs):
            total = some.shape[1]
            terms += dot(some, grads[head * total : (head + 1) * total, :], NN)
        return terms

    for pair in range(heads // 2):
        both = jnp.concatenate([flipped(2 * pair), flipped(2 * pair + 1)], 0)
        span = slice(pair * lanes, (pair + 1) * lanes)
        mine_ref[:, span] = both[:, :rows].T
        other_ref[:, span] = both[:, rows:].T.astype(jnp.bfloat16)


def end_body(query_ref, query_back_ref, total_ref, *refs):
    term_refs, (q_out, k_out, v_out, q_buf, kv_buf, sems) = refs[:-6], refs[-6:]
    width = k_out.shape[0]
    query = query_ref[...] + query_back_ref[...].astype(jnp.float32)
    q_buf[...] = query.astype(q_buf.dtype)
    copies = [pltpu.make_async_copy(q_buf, q_out, sems.at[0])]
    copies[0].start()
    total = total_ref[...]
    for ref in term_refs:
        total = total + ref[...].astype(jnp.float32)
    kv_buf[...] = total.astype(kv_buf.dtype)
    copies.append(pltpu.make_async_copy(kv_buf.at[:width, :], k_out, sems.at[1]))
    copies.append(pltpu.make_async_copy(kv_buf.at[width:, :], v_out, sems.at[2]))
    for copy in copies[1:]:
        copy.start()
    for copy in copies:
        copy.wait()


def in_vmem(count):
    return [pl.BlockSpec(memory_space=pltpu.VMEM) for _ in range(count)]


def held(*arrays, space=pltpu.VMEM):
    return [pltpu.with_memory_space_constraint(x, space) for x in arrays]


def grant(slabs, rows, lanes):
    return pltpu.CompilerParams(vmem_limit_bytes=(8 << 20) + 192 * slabs * rows * lanes)


def per_device(queries, keys, values, attn_out, out_grad, log_norm, doc_start):
    rows, features = queries.shape
    heads = log_norm.shape[0]
    width = keys.shape[1]
    lanes = 2 * width
    half = lax.axis_size("team") // 2
    steps = [2 * n for n in range(1, half)]

    def low(*dims):
        return pltpu.VMEM(dims, jnp.bfloat16)

    def full(*dims):
        return pltpu.VMEM(dims, jnp.float32)

    params = grant(max(2, half), rows, lanes)
    mine, loaded, loaded_out, loaded_log, loaded_begin = pl.pallas_call(
        load_body,
        out_shape=[
            low(lanes, rows),
            low(heads * (rows + 8), lanes),
            low(rows, features),
            full(heads, rows),
            pltpu.VMEM((1, rows), jnp.int32),
        ],
        in_specs=[pl.BlockSpec(memory_space=pltpu.HBM)] * 7,
        out_specs=in_vmem(5),
        scratch_shapes=[pltpu.SemaphoreType.DMA((heads + 5,))],
        compiler_params=params,
    )(
        *held(
            queries,
            out_grad,
            attn_out,
            log_norm,
            doc_start.reshape(1, rows),
            keys.T,
            values.T,
            space=pltpu.HBM,
        )
    )
    past = around(mine, "blk", 1)
    own_rows = pl.pallas_call(
        front_body,
        out_shape=low(heads * (rows + 8), lanes),
        in_specs=in_vmem(4),
        out_specs=in_vmem(1)[0],
        input_output_aliases={0: 0},
        compiler_params=params,
    )(*held(loaded, loaded_out, loaded_log, loaded_begin))
    front = (own_rows, exchanged(own_rows, "team", 1))
    seen = [skewed(mine, k, True) for k in steps]
    own_grads, total = pl.pallas_call(
        own_body,
        out_shape=[low(heads * rows, 2 * rows), full(lanes, rows)],
        in_specs=in_vmem(FRONT + 1),
        out_specs=in_vmem(2),
        compiler_params=params,
    )(*held(*front, mine))
    past_grads, past_piece = pl.pallas_call(
        past_body,
        out_shape=[low(heads * rows, 2 * rows), low(lanes, rows)],
        in_specs=in_vmem(FRONT + 1),
        out_specs=in_vmem(2),
        compiler_params=params,
    )(*held(*front, past))
    rest_grads, *sent = pl.pallas_call(
        functools.partial(rest_body, steps),
        out_shape=[low(heads * (half - 1) * rows, 2 * rows)] + [low(lanes, rows)] * (half - 1),
        in_specs=in_vmem(FRONT + half - 1),
        out_specs=in_vmem(half),
        compiler_params=params,
    )(*held(*front, *seen))
    query_mine, query_other = pl.pallas_call(
        functools.partial(query_body, 1 + half),
        out_shape=[full(rows, features), low(rows, features)],
        in_specs=in_vmem(4 + half),
        out_specs=in_vmem(2),
        compiler_params=params,
    )(*held(own_grads, past_grads, rest_grads, mine, past, *seen))
    query_back = exchanged(query_other, "team", 1)
    got = [around(past_piece, "blk", -1)]
    got += [skewed(piece, k, False) for k, piece in zip(steps, sent)]
    half_grad = jax.ShapeDtypeStruct((width, rows), jnp.bfloat16)
    query_grad, key_grad, value_grad = pl.pallas_call(
        end_body,
        out_shape=[
            jax.ShapeDtypeStruct((rows, features), jnp.bfloat16),
            half_grad,
            half_grad,
        ],
        in_specs=in_vmem(3 + len(got)),
        out_specs=[pl.BlockSpec(memory_space=pltpu.HBM)] * 3,
        scratch_shapes=[
            low(rows, features),
            low(lanes, rows),
            pltpu.SemaphoreType.DMA((3,)),
        ],
        compiler_params=params,
    )(*held(query_mine, query_back, total, *got))
    return (query_grad, key_grad.T, value_grad.T)


def solution(mesh):
    row = P(("blk", "team"), None)

    return jax.shard_map(
        per_device,
        mesh=mesh,
        in_specs=(row, row, row, row, row, P(None, ("blk", "team")), P(("blk", "team"))),
        out_specs=(row, row, row),
        check_vma=False,
    )
```

```python
import functools
import math

import jax
import jax.numpy as jnp
from jax import lax
from jax.experimental import pallas as pl
from jax.experimental.pallas import tpu as pltpu
from jax.sharding import PartitionSpec as P


NT = (((1,), (1,)), ((), ()))
NN = (((1,), (0,)), ((), ()))
FRONT = 2


def around(x, axis, by):
    count = lax.axis_size(axis)
    pairs = [(i, (i + by) % count) for i in range(count) if by > 0 or i + by >= 0]
    return lax.ppermute(x, axis, pairs)


def exchanged(x, axis, step):
    count = lax.axis_size(axis)
    return lax.ppermute(x, axis, [(i, i ^ step) for i in range(count)])


def skewed(x, step, out):
    team, blk = lax.axis_size("team"), lax.axis_size("blk")
    pairs = []
    for t in range(team):
        slot = t ^ step
        for b in range(blk):
            ahead = b + 1 if slot < t else b
            if ahead < blk:
                pairs.append((t * blk + b, slot * blk + ahead))
    if not out:
        pairs = [(there, here) for here, there in pairs]
    return lax.ppermute(x, ("team", "blk"), pairs)


def dot(a, b, dims):
    return lax.dot_general(a, b, dims, preferred_element_type=jnp.float32)


def half_turn(x, width):
    return jnp.concatenate([x[:, width:], x[:, :width]], 1)


def in_parts(x):
    high = x.astype(jnp.bfloat16).astype(jnp.float32)
    middle = (x - high).astype(jnp.bfloat16).astype(jnp.float32)
    return [high, middle, x - high - middle]


def load_body(q_in, g_in, o_in, log_in, begin_in, k_in, v_in, *refs):
    mine_ref, rows_ref, o_ref, log_ref, begin_ref, sems = refs
    rows, features = q_in.shape
    width, lanes = k_in.shape[0], rows_ref.shape[1]
    moves = [
        (k_in, mine_ref.at[:width, :]),
        (v_in, mine_ref.at[width:, :]),
        (o_in, o_ref),
        (log_in, log_ref),
        (begin_in, begin_ref),
    ]
    for n, source in enumerate((q_in, g_in)):
        for pair in range(features // lanes):
            at = n * (features // lanes) + pair
            target = rows_ref.at[at * rows : (at + 1) * rows, :]
            moves.append((source.at[:, pair * lanes : (pair + 1) * lanes], target))
    copies = [pltpu.make_async_copy(x, y, sems.at[n]) for n, (x, y) in enumerate(moves)]
    for copy in copies:
        copy.start()
    for copy in copies:
        copy.wait()


def front_body(rows_in, o_ref, log_ref, begin_ref, rows_ref):
    heads, rows = log_ref.shape
    pairs, lanes = heads // 2, rows_in.shape[1]
    width = lanes // 2
    first = pairs * rows
    cotangents = [rows_in[first + n * rows : first + (n + 1) * rows, :] for n in range(pairs)]
    cotangents = jnp.concatenate(cotangents, 1).astype(jnp.float32)
    prod = cotangents * o_ref[...].astype(jnp.float32)
    feature = lax.broadcasted_iota(jnp.int32, (heads, heads * width), 1)
    head_of = lax.broadcasted_iota(jnp.int32, (heads, heads * width), 0)
    pick = (feature // width == head_of).astype(jnp.bfloat16)
    high = prod.astype(jnp.bfloat16)
    rest = (prod - high.astype(jnp.float32)).astype(jnp.bfloat16)
    delta = dot(pick, high, NT) + dot(pick, rest, NT)
    begin = jnp.broadcast_to(begin_ref[...], (heads, rows))
    begins = [(begin >> 8).astype(jnp.float32), (begin & 255).astype(jnp.float32)]
    parts = in_parts(log_ref[...]) + in_parts(delta) + begins
    rows_ref[heads * rows :, :] = jnp.concatenate(parts, 0).astype(jnp.bfloat16)


def tile_terms(slab_refs, bases, front, grad_ref):
    lanes, rows = slab_refs[0].shape
    width = lanes // 2
    heads = front[0].shape[0] // (rows + 8)
    total = len(slab_refs) * rows
    spot = lax.axis_index("team")
    first_row = (lax.axis_index("blk") * lax.axis_size("team") + spot) * rows
    aux = [ref[heads * rows :, :].astype(jnp.float32) for ref in front]

    def of_rows(*parts):
        both = []
        for one in aux:
            both.append(sum(one[part * heads : (part + 1) * heads, :] for part in parts))
        return jnp.concatenate(both, 1)

    def pair_rows(number):
        return jnp.concatenate([ref[number * rows : (number + 1) * rows, :] for ref in front], 0)

    log_norm = of_rows(0, 1, 2)
    delta = of_rows(3, 4, 5)
    begin = of_rows(6)[:1].astype(jnp.int32) * 256 + of_rows(7)[:1].astype(jnp.int32) - first_row
    kv = jnp.concatenate([ref[...] for ref in slab_refs], 1).T
    low_key = lax.broadcasted_iota(jnp.int32, (total, lanes), 1) < width
    none = jnp.zeros_like(kv)
    k_low = jnp.where(low_key, kv * jnp.asarray(1.0 / math.sqrt(width), kv.dtype), none)
    v_high = jnp.where(low_key, none, kv)
    key_halves = jnp.concatenate([k_low, half_turn(k_low, width)], 0)
    value_halves = jnp.concatenate([half_turn(v_high, width), v_high], 0)
    inside = lax.broadcasted_iota(jnp.int32, (rows, 2 * rows), 0)
    key_pos = jnp.concatenate([inside + base for base in bases], 0)
    lane = lax.broadcasted_iota(jnp.int32, (1, 2 * rows), 1)
    row_pos = jnp.where(lane < rows, lane, lane + ((spot ^ 1) - spot - 1) * rows)
    allowed = (key_pos >= begin) & (key_pos <= row_pos)
    queries, cotangents, probs, grads = [], [], ([], []), ([], [])
    for pair in range(heads // 2):
        q_pair = pair_rows(pair)
        g_pair = pair_rows(heads // 2 + pair)
        queries.append(q_pair)
        cotangents.append(g_pair)
        scores = dot(key_halves, q_pair, NT)
        prob_grads = dot(value_halves, g_pair, NT)
        for half in range(2):
            span = slice(half * total, (half + 1) * total)
            head = 2 * pair + half
            shifted = scores[span] - log_norm[head : head + 1, :]
            weights = jnp.exp(jnp.where(allowed, shifted, -jnp.inf))
            score_grad = weights * (prob_grads[span] - delta[head : head + 1, :])
            low = score_grad.astype(jnp.bfloat16)
            grad_ref[head * total : (head + 1) * total, :] = low
            probs[half].append(weights.astype(jnp.bfloat16))
            grads[half].append(low)

    def summed(terms, rights):
        both = jnp.concatenate([jnp.concatenate(terms[half], 1) for half in range(2)], 0)
        both = dot(both, jnp.concatenate(rights, 0), NN)
        return both[:total], both[total:]

    key_even, key_odd = summed(grads, queries)
    value_even, value_odd = summed(probs, cotangents)
    factor = jnp.float32(1.0 / math.sqrt(width))
    low_key = lax.broadcasted_iota(jnp.int32, (total, lanes), 1) < width
    straight = jnp.where(low_key, key_even * factor, value_odd)
    turned = half_turn(jnp.where(low_key, value_even, key_odd * factor), width)
    return straight + turned


def slab_of(terms, number, rows):
    return terms[number * rows : (number + 1) * rows, :].T


def own_body(*refs):
    front, slab_ref, grad_ref, own_ref = refs[:FRONT], refs[FRONT], refs[-2], refs[-1]
    terms = tile_terms([slab_ref], [0], front, grad_ref)
    own_ref[...] = slab_of(terms, 0, slab_ref.shape[1])


def past_body(*refs):
    front, slab_ref, grad_ref, piece_ref = refs[:FRONT], refs[FRONT], refs[-2], refs[-1]
    rows = slab_ref.shape[1]
    has_past = lax.axis_index("blk") > 0

    @pl.when(has_past)
    def _():
        terms = tile_terms([slab_ref], [-lax.axis_size("team") * rows], front, grad_ref)
        piece_ref[...] = slab_of(terms, 0, rows).astype(jnp.bfloat16)

    @pl.when(jnp.logical_not(has_past))
    def _():
        grad_ref[...] = jnp.zeros_like(grad_ref)
        piece_ref[...] = jnp.zeros_like(piece_ref)


def rest_body(steps, *refs):
    count = len(steps)
    front, slab_refs = refs[:FRONT], refs[FRONT : FRONT + count]
    grad_ref, *piece_refs = refs[FRONT + count :]
    _, rows = slab_refs[0].shape
    spot = lax.axis_index("team")
    block = lax.axis_size("team")
    bases = []
    for step in steps:
        slot = spot ^ step
        bases.append((slot - spot - jnp.where(slot > spot, block, 0)) * rows)
    terms = tile_terms(slab_refs, bases, front, grad_ref)
    for n, piece_ref in enumerate(piece_refs):
        part = slab_of(terms, n, rows)
        piece_ref[...] = part.astype(jnp.bfloat16)


def query_body(count, *refs):
    grad_refs, slab_refs, (mine_ref, other_ref) = refs[:3], refs[3 : 3 + count], refs[3 + count :]
    lanes, rows = slab_refs[0].shape
    width = lanes // 2
    heads = mine_ref.shape[1] // width
    small = jnp.asarray(1.0 / math.sqrt(width), slab_refs[0].dtype)
    groups = (slab_refs[:1], slab_refs[1:2], slab_refs[2:])
    keys = [jnp.concatenate([ref[:width, :] for ref in some], 1) * small for some in groups]

    def flipped(head):
        terms = 0.0
        for some, grads in zip(keys, grad_refs):
            total = some.shape[1]
            terms += dot(some, grads[head * total : (head + 1) * total, :], NN)
        return terms

    for pair in range(heads // 2):
        both = jnp.concatenate([flipped(2 * pair), flipped(2 * pair + 1)], 0)
        span = slice(pair * lanes, (pair + 1) * lanes)
        mine_ref[:, span] = both[:, :rows].T
        other_ref[:, span] = both[:, rows:].T.astype(jnp.bfloat16)


def end_body(query_ref, query_back_ref, total_ref, *refs):
    term_refs, (q_out, k_out, v_out, q_buf, kv_buf, sems) = refs[:-6], refs[-6:]
    width = k_out.shape[0]
    query = query_ref[...] + query_back_ref[...].astype(jnp.float32)
    q_buf[...] = query.astype(q_buf.dtype)
    copies = [pltpu.make_async_copy(q_buf, q_out, sems.at[0])]
    copies[0].start()
    total = total_ref[...]
    for ref in term_refs:
        total = total + ref[...].astype(jnp.float32)
    kv_buf[...] = total.astype(kv_buf.dtype)
    copies.append(pltpu.make_async_copy(kv_buf.at[:width, :], k_out, sems.at[1]))
    copies.append(pltpu.make_async_copy(kv_buf.at[width:, :], v_out, sems.at[2]))
    for copy in copies[1:]:
        copy.start()
    for copy in copies:
        copy.wait()


def in_vmem(count):
    return [pl.BlockSpec(memory_space=pltpu.VMEM) for _ in range(count)]


def held(*arrays, space=pltpu.VMEM):
    return [pltpu.with_memory_space_constraint(x, space) for x in arrays]


def grant(slabs, rows, lanes):
    return pltpu.CompilerParams(vmem_limit_bytes=(8 << 20) + 192 * slabs * rows * lanes)


def per_device(queries, keys, values, attn_out, out_grad, log_norm, doc_start):
    rows, features = queries.shape
    heads = log_norm.shape[0]
    width = keys.shape[1]
    lanes = 2 * width
    half = lax.axis_size("team") // 2
    steps = [2 * n for n in range(1, half)]

    def low(*dims):
        return pltpu.VMEM(dims, jnp.bfloat16)

    def full(*dims):
        return pltpu.VMEM(dims, jnp.float32)

    params = grant(max(2, half), rows, lanes)
    mine, loaded, loaded_out, loaded_log, loaded_begin = pl.pallas_call(
        load_body,
        out_shape=[
            low(lanes, rows),
            low(heads * (rows + 8), lanes),
            low(rows, features),
            full(heads, rows),
            pltpu.VMEM((1, rows), jnp.int32),
        ],
        in_specs=[pl.BlockSpec(memory_space=pltpu.HBM)] * 7,
        out_specs=in_vmem(5),
        scratch_shapes=[pltpu.SemaphoreType.DMA((heads + 5,))],
        compiler_params=params,
    )(
        *held(
            queries,
            out_grad,
            attn_out,
            log_norm,
            doc_start.reshape(1, rows),
            keys.T,
            values.T,
            space=pltpu.HBM,
        )
    )
    past = around(mine, "blk", 1)
    own_rows = pl.pallas_call(
        front_body,
        out_shape=low(heads * (rows + 8), lanes),
        in_specs=in_vmem(4),
        out_specs=in_vmem(1)[0],
        input_output_aliases={0: 0},
        compiler_params=params,
    )(*held(loaded, loaded_out, loaded_log, loaded_begin))
    front = (own_rows, exchanged(own_rows, "team", 1))
    seen = [skewed(mine, k, True) for k in steps]
    own_grads, total = pl.pallas_call(
        own_body,
        out_shape=[low(heads * rows, 2 * rows), full(lanes, rows)],
        in_specs=in_vmem(FRONT + 1),
        out_specs=in_vmem(2),
        compiler_params=params,
    )(*held(*front, mine))
    past_grads, past_piece = pl.pallas_call(
        past_body,
        out_shape=[low(heads * rows, 2 * rows), low(lanes, rows)],
        in_specs=in_vmem(FRONT + 1),
        out_specs=in_vmem(2),
        compiler_params=params,
    )(*held(*front, past))
    rest_grads, *sent = pl.pallas_call(
        functools.partial(rest_body, steps),
        out_shape=[low(heads * (half - 1) * rows, 2 * rows)] + [low(lanes, rows)] * (half - 1),
        in_specs=in_vmem(FRONT + half - 1),
        out_specs=in_vmem(half),
        compiler_params=params,
    )(*held(*front, *seen))
    query_mine, query_other = pl.pallas_call(
        functools.partial(query_body, 1 + half),
        out_shape=[full(rows, features), low(rows, features)],
        in_specs=in_vmem(4 + half),
        out_specs=in_vmem(2),
        compiler_params=params,
    )(*held(own_grads, past_grads, rest_grads, mine, past, *seen))
    query_back = exchanged(query_other, "team", 1)
    got = [around(past_piece, "blk", -1)]
    got += [skewed(piece, k, False) for k, piece in zip(steps, sent)]
    half_grad = jax.ShapeDtypeStruct((width, rows), jnp.bfloat16)
    query_grad, key_grad, value_grad = pl.pallas_call(
        end_body,
        out_shape=[
            jax.ShapeDtypeStruct((rows, features), jnp.bfloat16),
            half_grad,
            half_grad,
        ],
        in_specs=in_vmem(3 + len(got)),
        out_specs=[pl.BlockSpec(memory_space=pltpu.HBM)] * 3,
        scratch_shapes=[
            low(rows, features),
            low(lanes, rows),
            pltpu.SemaphoreType.DMA((3,)),
        ],
        compiler_params=params,
    )(*held(query_mine, query_back, total, *got))
    return (query_grad, key_grad.T, value_grad.T)


def solution(mesh):
    row = P(("blk", "team"), None)

    return jax.shard_map(
        per_device,
        mesh=mesh,
        in_specs=(row, row, row, row, row, P(None, ("blk", "team")), P(("blk", "team"))),
        out_specs=(row, row, row),
        check_vma=False,
    )
```

```python
import functools
import math

import jax
import jax.numpy as jnp
from jax import lax
from jax.experimental import pallas as pl
from jax.experimental.pallas import tpu as pltpu
from jax.sharding import PartitionSpec as P


NT = (((1,), (1,)), ((), ()))
NN = (((1,), (0,)), ((), ()))
FRONT = 2


def around(x, axis, by):
    count = lax.axis_size(axis)
    pairs = [(i, (i + by) % count) for i in range(count) if by > 0 or i + by >= 0]
    return lax.ppermute(x, axis, pairs)


def exchanged(x, axis, step):
    count = lax.axis_size(axis)
    return lax.ppermute(x, axis, [(i, i ^ step) for i in range(count)])


def skewed(x, step, out):
    team, blk = lax.axis_size("team"), lax.axis_size("blk")
    pairs = []
    for t in range(team):
        slot = t ^ step
        for b in range(blk):
            ahead = b + 1 if slot < t else b
            if ahead < blk:
                pairs.append((t * blk + b, slot * blk + ahead))
    if not out:
        pairs = [(there, here) for here, there in pairs]
    return lax.ppermute(x, ("team", "blk"), pairs)


def dot(a, b, dims):
    return lax.dot_general(a, b, dims, preferred_element_type=jnp.float32)


def half_turn(x, width):
    return jnp.concatenate([x[:, width:], x[:, :width]], 1)


def in_parts(x):
    high = x.astype(jnp.bfloat16).astype(jnp.float32)
    middle = (x - high).astype(jnp.bfloat16).astype(jnp.float32)
    return [high, middle, x - high - middle]


def load_body(q_in, g_in, o_in, log_in, begin_in, k_in, v_in, *refs):
    mine_ref, rows_ref, o_ref, log_ref, begin_ref, sems = refs
    rows, features = q_in.shape
    width, lanes = k_in.shape[0], rows_ref.shape[1]
    moves = [
        (k_in, mine_ref.at[:width, :]),
        (v_in, mine_ref.at[width:, :]),
        (o_in, o_ref),
        (log_in, log_ref),
        (begin_in, begin_ref),
    ]
    for n, source in enumerate((q_in, g_in)):
        for pair in range(features // lanes):
            at = n * (features // lanes) + pair
            target = rows_ref.at[at * rows : (at + 1) * rows, :]
            moves.append((source.at[:, pair * lanes : (pair + 1) * lanes], target))
    copies = [pltpu.make_async_copy(x, y, sems.at[n]) for n, (x, y) in enumerate(moves)]
    for copy in copies:
        copy.start()
    for copy in copies:
        copy.wait()


def front_body(rows_in, o_ref, log_ref, begin_ref, rows_ref):
    heads, rows = log_ref.shape
    pairs, lanes = heads // 2, rows_in.shape[1]
    width = lanes // 2
    first = pairs * rows
    cotangents = [rows_in[first + n * rows : first + (n + 1) * rows, :] for n in range(pairs)]
    cotangents = jnp.concatenate(cotangents, 1).astype(jnp.float32)
    prod = cotangents * o_ref[...].astype(jnp.float32)
    feature = lax.broadcasted_iota(jnp.int32, (heads, heads * width), 1)
    head_of = lax.broadcasted_iota(jnp.int32, (heads, heads * width), 0)
    pick = (feature // width == head_of).astype(jnp.bfloat16)
    high = prod.astype(jnp.bfloat16)
    rest = (prod - high.astype(jnp.float32)).astype(jnp.bfloat16)
    delta = dot(pick, high, NT) + dot(pick, rest, NT)
    begin = jnp.broadcast_to(begin_ref[...], (heads, rows))
    begins = [(begin >> 8).astype(jnp.float32), (begin & 255).astype(jnp.float32)]
    parts = in_parts(log_ref[...]) + in_parts(delta) + begins
    rows_ref[heads * rows :, :] = jnp.concatenate(parts, 0).astype(jnp.bfloat16)


def tile_terms(slab_refs, bases, front, grad_ref):
    lanes, rows = slab_refs[0].shape
    width = lanes // 2
    heads = front[0].shape[0] // (rows + 8)
    total = len(slab_refs) * rows
    spot = lax.axis_index("team")
    first_row = (lax.axis_index("blk") * lax.axis_size("team") + spot) * rows
    aux = [ref[heads * rows :, :].astype(jnp.float32) for ref in front]

    def of_rows(*parts):
        both = []
        for one in aux:
            both.append(sum(one[part * heads : (part + 1) * heads, :] for part in parts))
        return jnp.concatenate(both, 1)

    def pair_rows(number):
        return jnp.concatenate([ref[number * rows : (number + 1) * rows, :] for ref in front], 0)

    log_norm = of_rows(0, 1, 2)
    delta = of_rows(3, 4, 5)
    begin = of_rows(6)[:1].astype(jnp.int32) * 256 + of_rows(7)[:1].astype(jnp.int32) - first_row
    kv = jnp.concatenate([ref[...] for ref in slab_refs], 1).T
    low_key = lax.broadcasted_iota(jnp.int32, (total, lanes), 1) < width
    none = jnp.zeros_like(kv)
    k_low = jnp.where(low_key, kv * jnp.asarray(1.0 / math.sqrt(width), kv.dtype), none)
    v_high = jnp.where(low_key, none, kv)
    key_halves = jnp.concatenate([k_low, half_turn(k_low, width)], 0)
    value_halves = jnp.concatenate([half_turn(v_high, width), v_high], 0)
    inside = lax.broadcasted_iota(jnp.int32, (rows, 2 * rows), 0)
    key_pos = jnp.concatenate([inside + base for base in bases], 0)
    lane = lax.broadcasted_iota(jnp.int32, (1, 2 * rows), 1)
    row_pos = jnp.where(lane < rows, lane, lane + ((spot ^ 1) - spot - 1) * rows)
    allowed = (key_pos >= begin) & (key_pos <= row_pos)
    queries, cotangents, probs, grads = [], [], ([], []), ([], [])
    for pair in range(heads // 2):
        q_pair = pair_rows(pair)
        g_pair = pair_rows(heads // 2 + pair)
        queries.append(q_pair)
        cotangents.append(g_pair)
        scores = dot(key_halves, q_pair, NT)
        prob_grads = dot(value_halves, g_pair, NT)
        for half in range(2):
            span = slice(half * total, (half + 1) * total)
            head = 2 * pair + half
            shifted = scores[span] - log_norm[head : head + 1, :]
            weights = jnp.exp(jnp.where(allowed, shifted, -jnp.inf))
            score_grad = weights * (prob_grads[span] - delta[head : head + 1, :])
            low = score_grad.astype(jnp.bfloat16)
            grad_ref[head * total : (head + 1) * total, :] = low
            probs[half].append(weights.astype(jnp.bfloat16))
            grads[half].append(low)

    def summed(terms, rights):
        both = jnp.concatenate([jnp.concatenate(terms[half], 1) for half in range(2)], 0)
        both = dot(both, jnp.concatenate(rights, 0), NN)
        return both[:total], both[total:]

    key_even, key_odd = summed(grads, queries)
    value_even, value_odd = summed(probs, cotangents)
    factor = jnp.float32(1.0 / math.sqrt(width))
    low_key = lax.broadcasted_iota(jnp.int32, (total, lanes), 1) < width
    straight = jnp.where(low_key, key_even * factor, value_odd)
    turned = half_turn(jnp.where(low_key, value_even, key_odd * factor), width)
    return straight + turned


def slab_of(terms, number, rows):
    return terms[number * rows : (number + 1) * rows, :]


def own_body(*refs):
    front, slab_ref, grad_ref, own_ref = refs[:FRONT], refs[FRONT], refs[-2], refs[-1]
    terms = tile_terms([slab_ref], [0], front, grad_ref)
    own_ref[...] = slab_of(terms, 0, slab_ref.shape[1])


def past_body(*refs):
    front, slab_ref, grad_ref, piece_ref = refs[:FRONT], refs[FRONT], refs[-2], refs[-1]
    rows = slab_ref.shape[1]
    has_past = lax.axis_index("blk") > 0

    @pl.when(has_past)
    def _():
        terms = tile_terms([slab_ref], [-lax.axis_size("team") * rows], front, grad_ref)
        piece_ref[...] = slab_of(terms, 0, rows).astype(jnp.bfloat16)

    @pl.when(jnp.logical_not(has_past))
    def _():
        grad_ref[...] = jnp.zeros_like(grad_ref)
        piece_ref[...] = jnp.zeros_like(piece_ref)


def rest_body(steps, *refs):
    count = len(steps)
    front, slab_refs = refs[:FRONT], refs[FRONT : FRONT + count]
    grad_ref, *piece_refs = refs[FRONT + count :]
    _, rows = slab_refs[0].shape
    spot = lax.axis_index("team")
    block = lax.axis_size("team")
    bases = []
    for step in steps:
        slot = spot ^ step
        bases.append((slot - spot - jnp.where(slot > spot, block, 0)) * rows)
    terms = tile_terms(slab_refs, bases, front, grad_ref)
    for n, piece_ref in enumerate(piece_refs):
        part = slab_of(terms, n, rows)
        piece_ref[...] = part.astype(jnp.bfloat16)


def query_body(count, *refs):
    grad_refs, slab_refs, (mine_ref, other_ref) = refs[:3], refs[3 : 3 + count], refs[3 + count :]
    lanes, rows = slab_refs[0].shape
    width = lanes // 2
    heads = mine_ref.shape[1] // width
    small = jnp.asarray(1.0 / math.sqrt(width), slab_refs[0].dtype)
    groups = (slab_refs[:1], slab_refs[1:2], slab_refs[2:])
    keys = [jnp.concatenate([ref[:width, :] for ref in some], 1) * small for some in groups]

    def flipped(head):
        terms = 0.0
        for some, grads in zip(keys, grad_refs):
            total = some.shape[1]
            terms += dot(some, grads[head * total : (head + 1) * total, :], NN)
        return terms

    for pair in range(heads // 2):
        both = jnp.concatenate([flipped(2 * pair), flipped(2 * pair + 1)], 0)
        span = slice(pair * lanes, (pair + 1) * lanes)
        mine_ref[:, span] = both[:, :rows].T
        other_ref[:, span] = both[:, rows:].T.astype(jnp.bfloat16)


def end_body(query_ref, query_back_ref, total_ref, *refs):
    term_refs, (q_out, k_out, v_out, q_buf, kv_buf, sems) = refs[:-6], refs[-6:]
    width = k_out.shape[0]
    query = query_ref[...] + query_back_ref[...].astype(jnp.float32)
    q_buf[...] = query.astype(q_buf.dtype)
    copies = [pltpu.make_async_copy(q_buf, q_out, sems.at[0])]
    copies[0].start()
    total = total_ref[...]
    for ref in term_refs:
        total = total + ref[...].astype(jnp.float32)
    kv_buf[...] = total.T.astype(kv_buf.dtype)
    copies.append(pltpu.make_async_copy(kv_buf.at[:width, :], k_out, sems.at[1]))
    copies.append(pltpu.make_async_copy(kv_buf.at[width:, :], v_out, sems.at[2]))
    for copy in copies[1:]:
        copy.start()
    for copy in copies:
        copy.wait()


def in_vmem(count):
    return [pl.BlockSpec(memory_space=pltpu.VMEM) for _ in range(count)]


def held(*arrays, space=pltpu.VMEM):
    return [pltpu.with_memory_space_constraint(x, space) for x in arrays]


def grant(slabs, rows, lanes):
    return pltpu.CompilerParams(vmem_limit_bytes=(8 << 20) + 192 * slabs * rows * lanes)


def per_device(queries, keys, values, attn_out, out_grad, log_norm, doc_start):
    rows, features = queries.shape
    heads = log_norm.shape[0]
    width = keys.shape[1]
    lanes = 2 * width
    half = lax.axis_size("team") // 2
    steps = [2 * n for n in range(1, half)]

    def low(*dims):
        return pltpu.VMEM(dims, jnp.bfloat16)

    def full(*dims):
        return pltpu.VMEM(dims, jnp.float32)

    params = grant(max(2, half), rows, lanes)
    mine, loaded, loaded_out, loaded_log, loaded_begin = pl.pallas_call(
        load_body,
        out_shape=[
            low(lanes, rows),
            low(heads * (rows + 8), lanes),
            low(rows, features),
            full(heads, rows),
            pltpu.VMEM((1, rows), jnp.int32),
        ],
        in_specs=[pl.BlockSpec(memory_space=pltpu.HBM)] * 7,
        out_specs=in_vmem(5),
        scratch_shapes=[pltpu.SemaphoreType.DMA((heads + 5,))],
        compiler_params=params,
    )(
        *held(
            queries,
            out_grad,
            attn_out,
            log_norm,
            doc_start.reshape(1, rows),
            keys.T,
            values.T,
            space=pltpu.HBM,
        )
    )
    past = around(mine, "blk", 1)
    own_rows = pl.pallas_call(
        front_body,
        out_shape=low(heads * (rows + 8), lanes),
        in_specs=in_vmem(4),
        out_specs=in_vmem(1)[0],
        input_output_aliases={0: 0},
        compiler_params=params,
    )(*held(loaded, loaded_out, loaded_log, loaded_begin))
    front = (own_rows, exchanged(own_rows, "team", 1))
    seen = [skewed(mine, k, True) for k in steps]
    own_grads, total = pl.pallas_call(
        own_body,
        out_shape=[low(heads * rows, 2 * rows), full(rows, lanes)],
        in_specs=in_vmem(FRONT + 1),
        out_specs=in_vmem(2),
        compiler_params=params,
    )(*held(*front, mine))
    past_grads, past_piece = pl.pallas_call(
        past_body,
        out_shape=[low(heads * rows, 2 * rows), low(rows, lanes)],
        in_specs=in_vmem(FRONT + 1),
        out_specs=in_vmem(2),
        compiler_params=params,
    )(*held(*front, past))
    rest_grads, *sent = pl.pallas_call(
        functools.partial(rest_body, steps),
        out_shape=[low(heads * (half - 1) * rows, 2 * rows)] + [low(rows, lanes)] * (half - 1),
        in_specs=in_vmem(FRONT + half - 1),
        out_specs=in_vmem(half),
        compiler_params=params,
    )(*held(*front, *seen))
    query_mine, query_other = pl.pallas_call(
        functools.partial(query_body, 1 + half),
        out_shape=[full(rows, features), low(rows, features)],
        in_specs=in_vmem(4 + half),
        out_specs=in_vmem(2),
        compiler_params=params,
    )(*held(own_grads, past_grads, rest_grads, mine, past, *seen))
    query_back = exchanged(query_other, "team", 1)
    got = [around(past_piece, "blk", -1)]
    got += [skewed(piece, k, False) for k, piece in zip(steps, sent)]
    half_grad = jax.ShapeDtypeStruct((width, rows), jnp.bfloat16)
    query_grad, key_grad, value_grad = pl.pallas_call(
        end_body,
        out_shape=[
            jax.ShapeDtypeStruct((rows, features), jnp.bfloat16),
            half_grad,
            half_grad,
        ],
        in_specs=in_vmem(3 + len(got)),
        out_specs=[pl.BlockSpec(memory_space=pltpu.HBM)] * 3,
        scratch_shapes=[
            low(rows, features),
            low(lanes, rows),
            pltpu.SemaphoreType.DMA((3,)),
        ],
        compiler_params=params,
    )(*held(query_mine, query_back, total, *got))
    return (query_grad, key_grad.T, value_grad.T)


def solution(mesh):
    row = P(("blk", "team"), None)

    return jax.shard_map(
        per_device,
        mesh=mesh,
        in_specs=(row, row, row, row, row, P(None, ("blk", "team")), P(("blk", "team"))),
        out_specs=(row, row, row),
        check_vma=False,
    )
```
